256 devices in a mesh: leaf: 32 (over z_lo, x, core), head: 8 (over z_hi, y).
Axes of the slice: x: 4, y: 4, z: 8 (z_hi: 2, z_lo: 4; z = z_hi * 4 + z_lo), core: 2. Of those that a mesh axis runs over, the one named last changes fastest.
Arguments:
- queries: bfloat16 [6144, 73728], P('leaf', 'head'), may hold values from -80 to 80
- d_out: bfloat16 [6144, 65536], P('leaf', 'head'), may hold values from -24 to 24
- branch_latent: bfloat16 [6144, 576], P('leaf'), may hold values from -6 to 6
- trunk_latent: bfloat16 [512, 8, 576], P('leaf'), may hold values from -6 to 6
- ancestors: int32 [32, 32], replicated, may hold values from 0 to 511, as said below
- anc_count: int32 [32], replicated, may hold values from 24 to 32, as said below
Outputs:
- d_queries: bfloat16 [6144, 73728], P('leaf', 'head')
- d_branch: float32 [6144, 576], P(('leaf', 'head'))
- d_trunk: float32 [512, 8, 576], P('leaf', 'head')
The draws below stay inside these ranges and needn't reach their ends.
Inputs may be any that keep to these rules, and one draw needn't show every extreme that they name: `ancestors`: each row lists 32 different trunk blocks; the owner of a block is its number // 16; a row lists 2 blocks of each owner that it names, never more. `anc_count`: some branch has all 32 slots live.
All inputs are finite; a program needn't handle non-finite values.
Results may differ from the reference program's by a relative error of at most 0.014.
Values may be sent and summed in bfloat16 or wider, within the bound.
A program may use at most 128 MiB of HBM per device.

```python
import jax
import jax.numpy as jnp
from jax import lax

HEADS = 128
RANK = 512
QK_HEAD = 192
LATENT = 576
BR_DEV = 192
BLK = 8
CAP = 2
ANC = 32
TRK_BLK = 16
TOKENS = 6144
TRUNK_BLOCKS = 512
N_LEAF = 32


def latent_field(key):
    base = jax.random.fold_in(key, 11)
    field = jax.random.normal(base, (TOKENS, LATENT), jnp.float32)
    return jnp.clip(field, -6.0, 6.0)


def draw_branch_latent(key, part):
    return latent_field(key).astype(jnp.bfloat16)


def draw_queries(key, part):
    sub = jax.random.fold_in(key, 23)
    base = jax.random.normal(sub, (TOKENS, HEADS, LATENT), jnp.float32)
    return jnp.clip(base, -80.0, 80.0).reshape(TOKENS, HEADS * LATENT).astype(jnp.bfloat16)


def draw_ancestors(key, part):
    row_keys = jax.random.split(jax.random.fold_in(key, 31), N_LEAF)

    def one_row(row_key):
        owner_key, block_key = jax.random.split(row_key)
        chosen = jax.random.permutation(owner_key, N_LEAF)[:ANC // CAP]
        group_keys = jax.random.split(block_key, ANC // CAP)
        local_picks = jax.vmap(lambda gk: jax.random.permutation(gk, TRK_BLK)[:CAP])(group_keys)
        return (chosen[:, None] * TRK_BLK + local_picks).reshape(ANC)
    return jax.vmap(one_row)(row_keys).astype(jnp.int32)


def draw_anc_count(key, part):
    dropped = jax.random.randint(jax.random.fold_in(key, 37), (N_LEAF,), 0, ANC // 4 + 1)
    full_at = jax.random.randint(jax.random.fold_in(key, 41), (), 0, N_LEAF)
    dropped = jnp.where(jnp.arange(N_LEAF, dtype=jnp.int32) == full_at, 0, dropped)
    return (ANC - dropped).astype(jnp.int32)


def block_levels(own_key, extent, shards, least, largest):
    def one(axis_at, shards_of):
        heights = jax.random.uniform(jax.random.fold_in(jax.random.fold_in(own_key, 6), axis_at), (shards_of,), jnp.float32, least / len(shards), largest / len(shards))
        return jnp.repeat(jnp.exp(heights), extent[axis_at] // shards_of).reshape((-1,) + (1,) * (len(extent) - axis_at - 1))

    loudness = one(*shards[0])
    for cut in shards[1:]:
        loudness = loudness * one(*cut)
    return loudness


def normal_values(rng, dims, spread, bound, pieces=(), kind=jnp.bfloat16):
    entries = spread * jax.random.normal(rng, dims, jnp.float32)
    if pieces:
        entries = entries * block_levels(rng, dims, pieces, -0.22, 0.18)
    return jnp.clip(entries, -bound, bound).astype(kind)


def setup_inputs(seed: int = 0) -> dict:
    splits = jax.random.split(jax.random.key(seed), 7)
    return {
        "queries": draw_queries(jax.random.fold_in(splits[6], 71), 0),
        "d_out": normal_values(splits[1], (TOKENS, HEADS * RANK), 4.0, 24.0, ((0, 32), (1, 8))),
        "branch_latent": draw_branch_latent(jax.random.fold_in(splits[6], 71), 0),
        "trunk_latent": normal_values(splits[3], (TRUNK_BLOCKS, BLK, LATENT), 1.0, 6.0, ((0, 32),)),
        "ancestors": draw_ancestors(jax.random.fold_in(splits[6], 71), 0),
        "anc_count": draw_anc_count(jax.random.fold_in(splits[6], 71), 0),
    }


def reference(queries, d_out, branch_latent, trunk_latent, ancestors, anc_count):
    score_scale = float(QK_HEAD) ** -0.5
    far_rows = ANC * BLK

    def one_branch(branch):
        start = branch * BR_DEV
        query_heads = lax.dynamic_slice_in_dim(queries, start, BR_DEV, 0).reshape(BR_DEV, HEADS, LATENT).astype(jnp.float32)
        grad_heads = lax.dynamic_slice_in_dim(d_out, start, BR_DEV, 0).reshape(BR_DEV, HEADS, RANK).astype(jnp.float32)
        own_rows = lax.dynamic_slice_in_dim(branch_latent, start, BR_DEV, 0)
        listed = ancestors[branch]
        own_count = anc_count[branch]
        far_data = jnp.take(trunk_latent, listed, axis=0).reshape(far_rows, LATENT)
        key_rows = jnp.concatenate([far_data, own_rows], axis=0).astype(jnp.float32)
        far_ok = (jnp.arange(far_rows, dtype=jnp.int32) // BLK) < own_count
        causal = jnp.arange(BR_DEV, dtype=jnp.int32)[None, :] <= jnp.arange(BR_DEV, dtype=jnp.int32)[:, None]
        allowed = jnp.concatenate([jnp.broadcast_to(far_ok[None, :], (BR_DEV, far_rows)), causal], axis=1)
        scores = jnp.einsum("thc,kc->htk", query_heads, key_rows) * score_scale
        scores = jnp.where(allowed[None], scores, -1e30)
        row_max = jnp.max(scores, axis=2, keepdims=True)
        expo = jnp.exp(scores - row_max)
        attn = expo / jnp.sum(expo, axis=2, keepdims=True)
        attn_low = lax.optimization_barrier(attn.astype(jnp.bfloat16)).astype(jnp.float32)
        d_prob = jnp.einsum("thr,kr->htk", grad_heads, key_rows[:, :RANK])
        row_delta = jnp.sum(attn * d_prob, axis=2, keepdims=True)
        d_score = lax.optimization_barrier((attn * (d_prob - row_delta)).astype(jnp.bfloat16)).astype(jnp.float32)
        d_query = (jnp.einsum("htk,kc->thc", d_score, key_rows) * score_scale).astype(jnp.bfloat16)
        d_key = jnp.einsum("htk,thc->kc", d_score, query_heads) * score_scale
        d_value = jnp.einsum("htk,thr->kr", attn_low, grad_heads)
        d_key = d_key + jnp.pad(d_value, ((0, 0), (0, LATENT - RANK)))
        return d_query.reshape(BR_DEV, HEADS * LATENT), d_key

    branches = jnp.arange(N_LEAF, dtype=jnp.int32)
    d_query_all, d_key_all = lax.map(one_branch, branches)
    d_queries = d_query_all.reshape(TOKENS, HEADS * LATENT)
    d_branch = d_key_all[:, far_rows:].reshape(TOKENS, LATENT)
    far_grad = d_key_all[:, :far_rows].reshape(N_LEAF * ANC, BLK, LATENT)
    d_trunk = jnp.zeros((TRUNK_BLOCKS, BLK, LATENT), jnp.float32).at[ancestors.reshape(-1)].add(far_grad)
    return d_queries, d_branch, d_trunk
```

```python
import functools

import jax
import jax.numpy as jnp
from jax import lax
from jax.experimental import pallas as pl
from jax.experimental.pallas import tpu as pltpu
from jax.sharding import PartitionSpec as P

F32, BF16 = jnp.float32, jnp.bfloat16
SCALE = float(192) ** -0.5
LOG2E = 1.4426950408889634
LEAF = 32
WIDE = 640


def dot(a, b, ca, cb):
    return lax.dot_general(a, b, (((ca,), (cb,)), ((), ())), preferred_element_type=F32)


def iota(shape, dim):
    return lax.broadcasted_iota(jnp.int32, shape, dim)


def listed_block(anc, leaf, branch, pick):
    rows = branch.shape[0]
    expand = (branch == iota((rows, LEAF), 1)).astype(F32).astype(BF16)
    owner = dot(expand, (anc >> 4).astype(F32).astype(BF16), 1, 0)
    local = dot(expand, (anc & 15).astype(F32).astype(BF16), 1, 0)
    mine = jnp.where(owner == leaf.astype(F32), 1.0, 0.0)
    before = jnp.where(iota((LEAF, LEAF), 0) < iota((LEAF, LEAF), 1), 1.0, 0.0).astype(BF16)
    rank = dot(mine.astype(BF16), before, 1, 0)
    chosen = jnp.where(rank == pick.astype(F32), mine, 0.0)
    return jnp.sum(chosen * (local + 1.0), axis=1, keepdims=True)


def owner_and_rank(row, slot):
    rows = slot.shape[0]
    owners = (row >> 4).astype(F32)
    at = iota((rows, LEAF), 1)
    owner = jnp.sum(jnp.where(at == slot, owners, 0.0), axis=1, keepdims=True)
    rank = jnp.sum(jnp.where((owners == owner) & (at < slot), 1.0, 0.0), axis=1, keepdims=True)
    return owner, rank


def remote(src, dst, send, recv, where):
    return pltpu.make_async_remote_copy(
        src_ref=src, dst_ref=dst, send_sem=send, recv_sem=recv, device_id=where, device_id_type=pl.DeviceIdType.MESH
    )


def signal(sem, where):
    pl.semaphore_signal(sem, inc=1, device_id=where, device_id_type=pl.DeviceIdType.MESH)


def gather(anc_ref, trunk_ref, keys_ref, out, got, tall, slabs, out_send, out_recv, ring_send, ring_recv):
    leaf, head = lax.axis_index("leaf"), lax.axis_index("head")
    deep, y = head // 4, lax.rem(head, 4)
    right = {"head": deep * 4 + lax.rem(y + 1, 4)}
    left = {"head": deep * 4 + lax.rem(y + 3, 4)}
    barrier = pltpu.get_barrier_semaphore()

    def greet(k, c):
        signal(barrier, {"leaf": lax.rem(leaf + k, LEAF)})
        return c

    lax.fori_loop(1, LEAF, greet, 0)
    signal(barrier, left)
    signal(barrier, right)

    i = iota((128, 1), 0)
    block = listed_block(anc_ref[...], leaf, i // 4, (i // 2) % 2)
    want = (block - 1.0) * 8.0 + (i % 2 + 2 * y).astype(F32)
    pick = jnp.where(want == iota((128, 128), 1).astype(F32), 1.0, 0.0).astype(BF16)
    trunk = trunk_ref[...].astype(F32).reshape(128, 576).astype(BF16)
    rows = dot(pick, jnp.concatenate([trunk, jnp.zeros((128, WIDE - 576), BF16)], axis=1), 1, 0)
    for b in range(LEAF):
        out[b] = rows[4 * b:4 * b + 4].astype(BF16)

    pl.semaphore_wait(barrier, LEAF + 1)

    def send(k, c):
        to = lax.rem(leaf + k, LEAF)
        remote(out.at[to], got.at[leaf], out_send.at[k], out_recv.at[leaf], {"leaf": to}).start()
        return c

    lax.fori_loop(1, LEAF, send, 0)
    mine = pltpu.make_async_copy(out.at[leaf], got.at[leaf], out_recv.at[leaf])
    mine.start()

    i = iota((64, 1), 0)
    owner, rank = owner_and_rank(anc_ref[pl.ds(leaf, 1), :], i % 32)
    want = owner * 4.0 + rank * 2.0 + (i // 32).astype(F32)
    pick = jnp.where(want == iota((64, 128), 1).astype(F32), 1.0, 0.0).astype(BF16)

    mine.wait()

    def receive(k, c):
        source = lax.rem(leaf + k, LEAF)
        remote(out.at[source], got.at[source], out_send.at[k], out_recv.at[source], {"leaf": source}).wait()
        return c

    lax.fori_loop(1, LEAF, receive, 0)
    for b in range(LEAF):
        tall[4 * b:4 * b + 4, :] = got[b].astype(F32)
    slabs[y] = dot(pick, tall[...].astype(BF16), 1, 0).astype(BF16)

    def hop(k, slab, half, where):
        part = slabs.at[slab, pl.ds(32 * half, 32)]
        return remote(part, part, ring_send.at[k], ring_recv.at[k], where)

    up, down = lax.rem(y + 3, 4), lax.rem(y + 1, 4)
    first = [hop(0, y, 0, right), hop(1, y, 1, left), hop(2, y, 1, right), hop(3, y, 0, left)]
    for copy in first:
        copy.start()
    hop(0, up, 0, right).wait_recv()
    pass_right = hop(4, up, 0, right)
    pass_right.start()
    hop(1, down, 1, left).wait_recv()
    pass_left = hop(5, down, 1, left)
    pass_left.start()
    far = lax.rem(y + 2, 4)
    hop(2, up, 1, right).wait_recv()
    hop(3, down, 0, left).wait_recv()
    hop(4, far, 0, right).wait_recv()
    hop(5, far, 1, left).wait_recv()
    for copy in first + [pass_right, pass_left]:
        copy.wait_send()
    for s in range(4):
        keys_ref[64 * s:64 * s + 64, :] = slabs[s]


def gather_call(ancestors, trunk):
    return pl.pallas_call(
        gather,
        out_shape=jax.ShapeDtypeStruct((256, WIDE), BF16),
        in_specs=[pl.BlockSpec(memory_space=pltpu.VMEM)] * 2,
        out_specs=pl.BlockSpec(memory_space=pltpu.VMEM),
        scratch_shapes=[
            pltpu.VMEM((LEAF, 4, WIDE), BF16),
            pltpu.VMEM((LEAF, 4, WIDE), BF16),
            pltpu.VMEM((128, WIDE), F32),
            pltpu.VMEM((4, 64, WIDE), BF16),
            pltpu.SemaphoreType.DMA((LEAF,)),
            pltpu.SemaphoreType.DMA((LEAF,)),
            pltpu.SemaphoreType.DMA((6,)),
            pltpu.SemaphoreType.DMA((6,)),
        ],
        compiler_params=pltpu.CompilerParams(collective_id=0, has_side_effects=True),
        name="gather",
    )(ancestors, trunk)


def attend(G, count_ref, far_ref, own_ref, q_ref, do_ref, dq_ref, dk_ref, ke, ko, bias, acc_e, acc_o, acc_v):
    step = pl.program_id(0)
    T = 192 * G
    @pl.when(step == 0)
    def _():
        ke[0:256, :] = far_ref[...]
        ke[256:448, :] = jnp.concatenate([own_ref[...], jnp.zeros((192, 64), BF16)], axis=1)
        ko[...] = pltpu.roll(ke[...].astype(F32), 64, 1).astype(BF16)
        row = lax.broadcasted_iota(jnp.int32, (256, 192), 0)
        bias[0:256, :] = jnp.where(row % 32 < count_ref[lax.axis_index("leaf")], 0.0, -1e30)
        row = lax.broadcasted_iota(jnp.int32, (192, 192), 0)
        col = lax.broadcasted_iota(jnp.int32, (192, 192), 1)
        bias[256:448, :] = jnp.where(row <= col, 0.0, -1e30)
        acc_e[...] = jnp.zeros_like(acc_e)
        acc_o[...] = jnp.zeros_like(acc_o)
        acc_v[...] = jnp.zeros_like(acc_v)
    for par in range(2):
        K = (ke, ko)[par][...]
        Q = jnp.concatenate([q_ref[:, 1152 * g + 512 * par:1152 * g + 512 * par + 640] for g in range(G)], axis=0)
        DO = jnp.concatenate([do_ref[:, 1024 * g + 512 * par:1024 * g + 512 * par + 512] for g in range(G)], axis=0)
        s = dot(K, Q, 1, 1)
        dp = dot(ke[:, 0:512], DO, 1, 1)
        b = bias[...]
        s = s + jnp.concatenate([b] * G, axis=1)
        m = jnp.max(s, axis=0, keepdims=True)
        e = jnp.exp2((s - m) * (SCALE * LOG2E))
        p = e * (1.0 / jnp.sum(e, axis=0, keepdims=True))
        delta = jnp.sum(p * dp, axis=0, keepdims=True)
        ds = (p * (dp - delta)).astype(BF16)
        acc_v[...] += dot(p.astype(BF16), DO, 1, 0)
        acc = (acc_e, acc_o)[par]
        acc[...] += dot(ds, Q, 1, 0)
        dq = dot(ds, K, 0, 0) * SCALE
        if par == 0:
            dqe = dq
        else:
            for g in range(G):
                r = slice(192 * g, 192 * g + 192)
                c = 1152 * g
                dq_ref[:, c:c + 512] = dqe[r, 0:512].astype(BF16)
                dq_ref[:, c + 512:c + 640] = (dqe[r, 512:640] + dq[r, 0:128]).astype(BF16)
                dq_ref[:, c + 640:c + 1152] = dq[r, 128:640].astype(BF16)
    @pl.when(step == pl.num_programs(0) - 1)
    def _():
        dk = (acc_e[...] + pltpu.roll(acc_o[...], 576, 1)) * SCALE
        acc_e[:, 0:512] = dk[:, 0:512] + acc_v[...]
        acc_e[:, 512:640] = dk[:, 512:640]
        for h in range(8):
            dk_ref[h, 0:32, :] = acc_e[32 * h:32 * h + 32, :].astype(BF16)
            dk_ref[h, 32:56, :] = acc_e[256 + 24 * h:280 + 24 * h, :].astype(BF16)


def attend_call(G, count, far, own, q, do):
    return pl.pallas_call(
        functools.partial(attend, G),
        grid=(8 // G,),
        out_shape=(jax.ShapeDtypeStruct((192, 9216), BF16), jax.ShapeDtypeStruct((8, 56, 640), BF16)),
        in_specs=[pl.BlockSpec(memory_space=pltpu.SMEM),
                  pl.BlockSpec((256, 640), lambda i: (0, 0)), pl.BlockSpec((192, 576), lambda i: (0, 0)),
                  pl.BlockSpec((192, 1152 * G), lambda i: (0, i)), pl.BlockSpec((192, 1024 * G), lambda i: (0, i))],
        out_specs=(pl.BlockSpec((192, 1152 * G), lambda i: (0, i)), pl.BlockSpec((8, 56, 640), lambda i: (0, 0, 0))),
        scratch_shapes=[pltpu.VMEM((448, 640), BF16)] * 2 + [pltpu.VMEM((448, 192), F32)]
        + [pltpu.VMEM((448, 640), F32)] * 2 + [pltpu.VMEM((448, 512), F32)],
        name="attend",
    )(count, far, own, q, do)


def reduce(anc_ref, dk_ref, branch_ref, trunk_ref, near, pair, pair_in, out, got, tall,
           near_send, near_recv, pair_send, pair_recv, out_send, out_recv):
    leaf, head = lax.axis_index("leaf"), lax.axis_index("head")
    deep, y = head // 4, lax.rem(head, 4)
    me = deep * LEAF + leaf
    barrier = pltpu.get_barrier_semaphore()

    def plane(p):
        return {"leaf": lax.rem(p, LEAF), "head": (p // LEAF) * 4 + y}

    def greet(k, c):
        signal(barrier, plane(lax.rem(me + k, 2 * LEAF)))
        return c

    lax.fori_loop(1, 2 * LEAF, greet, 0)
    for k in range(1, 4):
        signal(barrier, {"head": deep * 4 + lax.rem(y + k, 4)})

    i = iota((64, 1), 0)
    owner, rank = owner_and_rank(anc_ref[pl.ds(leaf, 1), :], i % 32)
    want = (i // 32).astype(F32) * 64.0 + owner * 2.0 + rank
    spread = jnp.where(want == iota((64, 128), 1).astype(F32), 1.0, 0.0).astype(BF16)
    i = iota((128, 1), 0)
    block = listed_block(anc_ref[...], leaf, (i // 2) % 32, i % 2)
    collect = jnp.where(block - 1.0 == iota((128, 16), 1).astype(F32), 1.0, 0.0).astype(BF16)

    pl.semaphore_wait(barrier, 2 * LEAF + 2)

    def sent(part, rows, k, half):
        to = lax.rem(y + k, 4)
        n = part * 8 + half * 4 + k
        return remote(dk_ref.at[half * 4 + to, rows], near.at[k, half, rows], near_send.at[n], near_recv.at[n],
                      {"head": deep * 4 + to})

    parts = (pl.ds(0, 32), pl.ds(32, 24))
    copies = [[sent(part, parts[part], k, half) for k in (2, 1, 3) for half in range(2)] for part in range(2)]
    for copy in copies[0] + copies[1]:
        copy.start()
    for copy in copies[0]:
        copy.wait_recv()
    sums = []
    for half in range(2):
        total = dk_ref[half * 4 + y, 0:32, :].astype(F32)
        for k in range(1, 4):
            total = total + near[k, half, 0:32, :].astype(F32)
        sums.append(total.astype(BF16))
    rows = dot(spread, jnp.concatenate(sums, axis=0), 0, 0)
    for d in range(2 * LEAF):
        out[d] = rows[2 * d:2 * d + 2].astype(BF16)

    def send(k, c):
        to = lax.rem(me + k, 2 * LEAF)
        remote(out.at[to], got.at[me], out_send.at[k], out_recv.at[me], plane(to)).start()
        return c

    lax.fori_loop(1, 2 * LEAF, send, 0)
    mine = pltpu.make_async_copy(out.at[me], got.at[me], out_recv.at[me])
    mine.start()

    for copy in copies[1]:
        copy.wait_recv()
    for half in range(2):
        total = dk_ref[half * 4 + y, 32:56, :].astype(F32)
        for k in range(1, 4):
            total = total + near[k, half, 32:56, :].astype(F32)
        pair[half] = total
    pair_out = remote(pair.at[1 - deep], pair_in, pair_send, pair_recv, {"head": (1 - deep) * 4 + y})
    pair_out.start()

    mine.wait()

    def receive(k, c):
        source = lax.rem(me + k, 2 * LEAF)
        remote(out.at[source], got.at[source], out_send.at[k], out_recv.at[source], plane(source)).wait()
        return c

    lax.fori_loop(1, 2 * LEAF, receive, 0)
    for d in range(2 * LEAF):
        tall[2 * d:2 * d + 2, :] = got[d].astype(F32)
    trunk_ref[...] = dot(collect, tall[...].astype(BF16), 0, 0)[:, 0:576]
    pair_out.wait()
    branch_ref[...] = (pair[deep] + pair_in[...])[:, 0:576]
    for copy in copies[0] + copies[1]:
        copy.wait_send()


def reduce_call(ancestors, dk):
    return pl.pallas_call(
        reduce,
        out_shape=(jax.ShapeDtypeStruct((24, 576), F32), jax.ShapeDtypeStruct((16, 576), F32)),
        in_specs=[pl.BlockSpec(memory_space=pltpu.VMEM)] * 2,
        out_specs=(pl.BlockSpec(memory_space=pltpu.VMEM),) * 2,
        scratch_shapes=[
            pltpu.VMEM((4, 2, 56, WIDE), BF16),
            pltpu.VMEM((2, 24, WIDE), F32),
            pltpu.VMEM((24, WIDE), F32),
            pltpu.VMEM((2 * LEAF, 2, WIDE), BF16),
            pltpu.VMEM((2 * LEAF, 2, WIDE), BF16),
            pltpu.VMEM((128, WIDE), F32),
            pltpu.SemaphoreType.DMA((16,)),
            pltpu.SemaphoreType.DMA((16,)),
            pltpu.SemaphoreType.DMA,
            pltpu.SemaphoreType.DMA,
            pltpu.SemaphoreType.DMA((2 * LEAF,)),
            pltpu.SemaphoreType.DMA((2 * LEAF,)),
        ],
        compiler_params=pltpu.CompilerParams(collective_id=1, has_side_effects=True),
        name="reduce",
    )(ancestors, dk)


def local(queries, d_out, branch_latent, trunk_latent, ancestors, anc_count):
    far = gather_call(ancestors, trunk_latent)
    d_queries, dk = attend_call(4, anc_count, far, branch_latent, queries, d_out)
    d_branch, d_trunk = reduce_call(ancestors, dk)
    return d_queries, d_branch, d_trunk[:, None, :]


def solution(mesh):
    return jax.shard_map(
        local,
        mesh=mesh,
        in_specs=(P("leaf", "head"), P("leaf", "head"), P("leaf", None), P("leaf", None, None), P(), P()),
        out_specs=(P("leaf", "head"), P(("leaf", "head"), None), P("leaf", "head", None)),
        check_vma=False,
    )
```

```python
import functools

import jax
import jax.numpy as jnp
from jax import lax
from jax.experimental import pallas as pl
from jax.experimental.pallas import tpu as pltpu
from jax.sharding import PartitionSpec as P

F32, BF16 = jnp.float32, jnp.bfloat16
SCALE = float(192) ** -0.5
LOG2E = 1.4426950408889634
LEAF = 32
WIDE = 640


def dot(a, b, ca, cb):
    return lax.dot_general(a, b, (((ca,), (cb,)), ((), ())), preferred_element_type=F32)


def iota(shape, dim):
    return lax.broadcasted_iota(jnp.int32, shape, dim)


def listed_block(anc, leaf, branch, pick):
    rows = branch.shape[0]
    expand = (branch == iota((rows, LEAF), 1)).astype(F32).astype(BF16)
    owner = dot(expand, (anc >> 4).astype(F32).astype(BF16), 1, 0)
    local = dot(expand, (anc & 15).astype(F32).astype(BF16), 1, 0)
    mine = jnp.where(owner == leaf.astype(F32), 1.0, 0.0)
    before = jnp.where(iota((LEAF, LEAF), 0) < iota((LEAF, LEAF), 1), 1.0, 0.0).astype(BF16)
    rank = dot(mine.astype(BF16), before, 1, 0)
    chosen = jnp.where(rank == pick.astype(F32), mine, 0.0)
    return jnp.sum(chosen * (local + 1.0), axis=1, keepdims=True)


def owner_and_rank(row, slot):
    rows = slot.shape[0]
    owners = (row >> 4).astype(F32)
    at = iota((rows, LEAF), 1)
    owner = jnp.sum(jnp.where(at == slot, owners, 0.0), axis=1, keepdims=True)
    rank = jnp.sum(jnp.where((owners == owner) & (at < slot), 1.0, 0.0), axis=1, keepdims=True)
    return owner, rank


def remote(src, dst, send, recv, where):
    return pltpu.make_async_remote_copy(
        src_ref=src, dst_ref=dst, send_sem=send, recv_sem=recv, device_id=where, device_id_type=pl.DeviceIdType.MESH
    )


def signal(sem, where):
    pl.semaphore_signal(sem, inc=1, device_id=where, device_id_type=pl.DeviceIdType.MESH)


def fused(comm, anc_ref, cnt_ref, own_ref, trunk_ref, q_hbm, do_hbm, dq_hbm, branch_ref, spare_ref,
          qs, dos, keys, sown, dpown, p_own, ds, acc_k, acc_v, dq_out,
          g_out, g_got, g_tall, slabs, x_far, x_own, r_far, r_own, m_far, m_own, pair, pair_in, t_out, t_got, t_tall,
          load_sem, store_sem, g_send, g_recv, ring_send, ring_recv, far_send, far_recv, own_send, own_recv,
          pair_sem, t_send, t_recv):
    if comm:
        leaf, head = lax.axis_index("leaf"), lax.axis_index("head")
        deep, y = head // 4, lax.rem(head, 4)
        me = deep * LEAF + leaf
        right = {"head": deep * 4 + lax.rem(y + 1, 4)}
        left = {"head": deep * 4 + lax.rem(y + 3, 4)}

        def plane(p):
            return {"leaf": lax.rem(p, LEAF), "head": (p // LEAF) * 4 + y}

        barrier = pltpu.get_barrier_semaphore()

        def greet(k, c):
            signal(barrier, plane(lax.rem(me + k, 2 * LEAF)))
            return c

        lax.fori_loop(1, 2 * LEAF, greet, 0)
        signal(barrier, left)
        signal(barrier, right)
    else:
        leaf = 0

    loads = {}
    for u in range(2):
        for par in range(2):
            group = []
            for n in range(4):
                h = 4 * u + n
                at = pl.ds(192 * h, 192)
                k = 16 * u + 8 * par + 2 * n
                group.append(pltpu.make_async_copy(
                    q_hbm.at[:, pl.ds(1152 * h + 512 * par, WIDE)], qs.at[par, at], load_sem.at[k]))
                group.append(pltpu.make_async_copy(
                    do_hbm.at[:, pl.ds(1024 * h + 512 * par, 512)], dos.at[par, at], load_sem.at[k + 1]))
            for copy in group:
                copy.start()
            loads[u, par] = group
    chunks = [(u, par) for u in range(2) for par in range(2)]

    def q_of(u, par):
        return qs[par, 768 * u:768 * u + 768, :]

    def do_of(u, par):
        return dos[par, 768 * u:768 * u + 768, :]

    if comm:
        i = iota((128, 1), 0)
        block = listed_block(anc_ref[...], leaf, i // 4, (i // 2) % 2)
        want = (block - 1.0) * 8.0 + (4 * (i % 2) + y).astype(F32)
        pick = jnp.where(want == iota((128, 128), 1).astype(F32), 1.0, 0.0).astype(BF16)
        trunk = trunk_ref[...].astype(F32).reshape(128, 576).astype(BF16)
        rows = dot(pick, jnp.concatenate([trunk, jnp.zeros((128, WIDE - 576), BF16)], axis=1), 1, 0)
        for b in range(LEAF):
            g_out[b] = rows[4 * b:4 * b + 4].astype(BF16)
        i = iota((64, 1), 0)
        owner, rank = owner_and_rank(anc_ref[pl.ds(leaf, 1), :], i % 32)
        want = owner * 4.0 + rank * 2.0 + (i // 32).astype(F32)
        take = jnp.where(want == iota((64, 128), 1).astype(F32), 1.0, 0.0).astype(BF16)
        want = (i // 32).astype(F32) * 64.0 + owner * 2.0 + rank
        spread = jnp.where(want == iota((64, 128), 1).astype(F32), 1.0, 0.0).astype(BF16)
        i = iota((128, 1), 0)
        block = listed_block(anc_ref[...], leaf, (i // 2) % 32, i % 2)
        collect = jnp.where(block - 1.0 == iota((128, 16), 1).astype(F32), 1.0, 0.0).astype(BF16)

    own = own_ref[...]
    blank = jnp.zeros((192, 64), BF16)
    keys[0, 0:192, :] = jnp.concatenate([own, blank], axis=1)
    keys[1, 0:192, :] = pltpu.roll(jnp.concatenate([own, blank], axis=1).astype(F32), 64, 1).astype(BF16)
    causal = jnp.where(iota((192, 192), 0) <= iota((192, 192), 1), 0.0, -1e30)

    def own_scores(c):
        for copy in loads[chunks[c]]:
            copy.wait()
        u, par = chunks[c]
        s = dot(keys[par, 0:192, :], q_of(u, par), 1, 1)
        sown[c] = s + jnp.concatenate([causal] * 4, axis=1)
        dpown[c] = dot(keys[0, 0:192, 0:512], do_of(u, par), 1, 1)

    if comm:
        pl.semaphore_wait(barrier, 2 * LEAF + 1)

        def send(k, c):
            to = lax.rem(leaf + k, LEAF)
            remote(g_out.at[to], g_got.at[leaf], g_send.at[k], g_recv.at[leaf], {"leaf": to}).start()
            return c

        lax.fori_loop(1, LEAF, send, 0)
        mine = pltpu.make_async_copy(g_out.at[leaf], g_got.at[leaf], g_recv.at[leaf])
        mine.start()
        for c in range(4):
            own_scores(c)
        mine.wait()

        def receive(k, c):
            source = lax.rem(leaf + k, LEAF)
            remote(g_out.at[source], g_got.at[source], g_send.at[k], g_recv.at[source], {"leaf": source}).wait()
            return c

        lax.fori_loop(1, LEAF, receive, 0)
        for b in range(LEAF):
            g_tall[4 * b:4 * b + 4, :] = g_got[b].astype(F32)
        slabs[y] = dot(take, g_tall[...].astype(BF16), 1, 0).astype(BF16)

        def hop(k, slab, half, where):
            part = slabs.at[slab, pl.ds(32 * half, 32)]
            return remote(part, part, ring_send.at[k], ring_recv.at[k], where)

        up, down, far = lax.rem(y + 3, 4), lax.rem(y + 1, 4), lax.rem(y + 2, 4)
        ring = [hop(0, y, 0, right), hop(1, y, 1, left), hop(2, y, 1, right), hop(3, y, 0, left)]
        for copy in ring:
            copy.start()
        hop(0, up, 0, right).wait_recv()
        ring.append(hop(4, up, 0, right))
        ring[4].start()
        hop(1, down, 1, left).wait_recv()
        ring.append(hop(5, down, 1, left))
        ring[5].start()
        hop(2, up, 1, right).wait_recv()
        hop(3, down, 0, left).wait_recv()
        hop(4, far, 0, right).wait_recv()
        hop(5, far, 1, left).wait_recv()
        for k in range(4):
            keys[0, 192 + 64 * k:256 + 64 * k, :] = slabs[lax.rem(y + k, 4)]
    else:
        for c in range(4):
            own_scores(c)
        keys[0, 192:448, :] = trunk_ref[...]
    keys[1, 192:448, :] = pltpu.roll(keys[0, 192:448, :].astype(F32), 64, 1).astype(BF16)
    live = jnp.where(iota((256, 1), 0) % 32 < cnt_ref[leaf], 0.0, -1e30)

    def far_scores(c):
        u, par = chunks[c]
        return (dot(keys[par, 192:448, :], q_of(u, par), 1, 1) + live,
                dot(keys[0, 192:448, 0:512], do_of(u, par), 1, 1))

    ahead = far_scores(0)
    for c in range(4):
        u, par = chunks[c]
        sf, dpf = ahead
        if c < 3:
            ahead = far_scores(c + 1)
        so, dpo = sown[c], dpown[c]
        m = jnp.maximum(jnp.max(sf, axis=0, keepdims=True), jnp.max(so, axis=0, keepdims=True))
        ef = jnp.exp2((sf - m) * (SCALE * LOG2E))
        eo = jnp.exp2((so - m) * (SCALE * LOG2E))
        inv = 1.0 / (jnp.sum(ef, axis=0, keepdims=True) + jnp.sum(eo, axis=0, keepdims=True))
        pf, po = ef * inv, eo * inv
        delta = jnp.sum(pf * dpf, axis=0, keepdims=True) + jnp.sum(po * dpo, axis=0, keepdims=True)
        dsf = (pf * (dpf - delta)).astype(BF16)
        ds[c, 192:448, :] = dsf
        ds[c, 0:192, :] = (po * (dpo - delta)).astype(BF16)
        p_own[c] = po.astype(BF16)
        dk = dot(dsf, q_of(u, par), 1, 0)
        dv = dot(pf.astype(BF16), do_of(u, par), 1, 0)
        if u == 0:
            acc_k[par, 192:448, :] = dk
        else:
            acc_k[par, 192:448, :] += dk
        if c == 0:
            acc_v[192:448, :] = dv
        else:
            acc_v[192:448, :] += dv

    def merged(lo, n):
        dk = (acc_k[0, lo:lo + n, :] + pltpu.roll(acc_k[1, lo:lo + n, :], 576, 1)) * SCALE
        return jnp.concatenate([dk[:, 0:512] + acc_v[lo:lo + n, :], dk[:, 512:WIDE]], axis=1)

    for k in range(4):
        for half in range(2):
            x_far[k, half] = merged(192 + 64 * k + 32 * half, 32).astype(BF16)

    def ring_start(x, mid, send_sem, recv_sem):
        copies = [
            remote(x(2, 0), mid.at[0], send_sem.at[0], recv_sem.at[0], right),
            remote(x(2, 1), mid.at[1], send_sem.at[1], recv_sem.at[1], left),
            remote(x(1, 1), mid.at[2], send_sem.at[2], recv_sem.at[2], right),
            remote(x(3, 0), mid.at[3], send_sem.at[3], recv_sem.at[3], left),
        ]
        for copy in copies:
            copy.start()
        return copies

    def ring_pass(copies, value, mid, through, send_sem, recv_sem):
        for side, k in ((0, 1), (1, 3)):
            copies[side].wait_recv()
            through[side] = (value(k, side) + mid[side].astype(F32)).astype(BF16)
            copy = remote(through.at[side], mid.at[4 + side], send_sem.at[4 + side], recv_sem.at[4 + side],
                          (right, left)[side])
            copy.start()
            copies.append(copy)

    def ring_sum(copies, value, mid):
        for k in range(2, 6):
            copies[k].wait_recv()
        return [value(0, half) + mid[4 + half].astype(F32) + mid[3 - half].astype(F32) for half in range(2)]

    if comm:
        far_copies = ring_start(lambda k, half: x_far.at[k, half], r_far, far_send, far_recv)

    for c in range(4):
        u, par = chunks[c]
        dk = dot(ds[c, 0:192, :], q_of(u, par), 1, 0)
        dv = dot(p_own[c], do_of(u, par), 1, 0)
        if u == 0:
            acc_k[par, 0:192, :] = dk
        else:
            acc_k[par, 0:192, :] += dk
        if c == 0:
            acc_v[0:192, :] = dv
        else:
            acc_v[0:192, :] += dv
    for h in range(8):
        x_own[h] = merged(24 * h, 24).astype(BF16)

    def far_value(k, half):
        return x_far[k, half].astype(F32)

    def own_at(k, half):
        return half * 4 + lax.rem(y + k, 4)

    def own_value(k, half):
        return x_own[own_at(k, half)].astype(F32)

    def d_query(u):
        grads = [dot(ds[2 * u + par], keys[par], 0, 0) * SCALE for par in range(2)]
        for n in range(4):
            r = slice(192 * n, 192 * n + 192)
            at = 1152 * n
            dq_out[u, :, at:at + 512] = grads[0][r, 0:512].astype(BF16)
            dq_out[u, :, at + 512:at + 640] = (grads[0][r, 512:640] + grads[1][r, 0:128]).astype(BF16)
            dq_out[u, :, at + 640:at + 1152] = grads[1][r, 128:640].astype(BF16)
        copy = pltpu.make_async_copy(dq_out.at[u], dq_hbm.at[:, pl.ds(4608 * u, 4608)], store_sem.at[u])
        copy.start()
        return copy

    if comm:
        ring_pass(far_copies, far_value, r_far, m_far, far_send, far_recv)
        own_copies = ring_start(lambda k, half: x_own.at[own_at(k, half)], r_own, own_send, own_recv)
        stores = [d_query(0)]
        sums = ring_sum(far_copies, far_value, r_far)
        rows = dot(spread, jnp.concatenate(sums, axis=0).astype(BF16), 0, 0)
        for d in range(2 * LEAF):
            t_out[d] = rows[2 * d:2 * d + 2].astype(BF16)

        def send_rows(k, c):
            to = lax.rem(me + k, 2 * LEAF)
            remote(t_out.at[to], t_got.at[me], t_send.at[k], t_recv.at[me], plane(to)).start()
            return c

        lax.fori_loop(1, 2 * LEAF, send_rows, 0)
        mine = pltpu.make_async_copy(t_out.at[me], t_got.at[me], t_recv.at[me])
        mine.start()
        ring_pass(own_copies, own_value, r_own, m_own, own_send, own_recv)
        stores.append(d_query(1))
        sums = ring_sum(own_copies, own_value, r_own)
        for half in range(2):
            pair[half] = sums[half]
        pair_out = remote(pair.at[1 - deep], pair_in, pair_sem.at[0], pair_sem.at[1], {"head": (1 - deep) * 4 + y})
        pair_out.start()
        mine.wait()

        def receive_rows(k, c):
            source = lax.rem(me + k, 2 * LEAF)
            remote(t_out.at[source], t_got.at[source], t_send.at[k], t_recv.at[source], plane(source)).wait()
            return c

        lax.fori_loop(1, 2 * LEAF, receive_rows, 0)
        for d in range(2 * LEAF):
            t_tall[2 * d:2 * d + 2, :] = t_got[d].astype(F32)
        spare_ref[...] = dot(collect, t_tall[...].astype(BF16), 0, 0)[:, 0:576]
        pair_out.wait()
        branch_ref[...] = (pair[deep] + pair_in[...])[:, 0:576]
        for copy in ring + far_copies + own_copies:
            copy.wait_send()
    else:
        stores = [d_query(0), d_query(1)]
        spare_ref[...] = x_far[...]
        branch_ref[...] = x_own[...]
    for copy in stores:
        copy.wait()


def fused_call(comm, ancestors, count, own, trunk, q, do):
    if comm:
        small = (jax.ShapeDtypeStruct((24, 576), F32), jax.ShapeDtypeStruct((16, 576), F32))
    else:
        small = (jax.ShapeDtypeStruct((8, 24, WIDE), BF16), jax.ShapeDtypeStruct((4, 2, 32, WIDE), BF16))
    vmem, hbm = pl.BlockSpec(memory_space=pltpu.VMEM), pl.BlockSpec(memory_space=pl.ANY)
    dma = pltpu.SemaphoreType.DMA
    return pl.pallas_call(
        functools.partial(fused, comm),
        out_shape=(jax.ShapeDtypeStruct((192, 9216), BF16),) + small,
        in_specs=[vmem, pl.BlockSpec(memory_space=pltpu.SMEM), vmem, vmem, hbm, hbm],
        out_specs=(hbm, vmem, vmem),
        scratch_shapes=[
            pltpu.VMEM((2, 1536, WIDE), BF16),
            pltpu.VMEM((2, 1536, 512), BF16),
            pltpu.VMEM((2, 448, WIDE), BF16),
            pltpu.VMEM((4, 192, 768), F32),
            pltpu.VMEM((4, 192, 768), F32),
            pltpu.VMEM((4, 192, 768), BF16),
            pltpu.VMEM((4, 448, 768), BF16),
            pltpu.VMEM((2, 448, WIDE), F32),
            pltpu.VMEM((448, 512), F32),
            pltpu.VMEM((2, 192, 4608), BF16),
            pltpu.VMEM((LEAF, 4, WIDE), BF16),
            pltpu.VMEM((LEAF, 4, WIDE), BF16),
            pltpu.VMEM((128, WIDE), F32),
            pltpu.VMEM((4, 64, WIDE), BF16),
            pltpu.VMEM((4, 2, 32, WIDE), BF16),
            pltpu.VMEM((8, 24, WIDE), BF16),
            pltpu.VMEM((6, 32, WIDE), BF16),
            pltpu.VMEM((6, 24, WIDE), BF16),
            pltpu.VMEM((2, 32, WIDE), BF16),
            pltpu.VMEM((2, 24, WIDE), BF16),
            pltpu.VMEM((2, 24, WIDE), F32),
            pltpu.VMEM((24, WIDE), F32),
            pltpu.VMEM((2 * LEAF, 2, WIDE), BF16),
            pltpu.VMEM((2 * LEAF, 2, WIDE), BF16),
            pltpu.VMEM((128, WIDE), F32),
            dma((32,)), dma((2,)), dma((LEAF,)), dma((LEAF,)), dma((6,)), dma((6,)), dma((6,)), dma((6,)),
            dma((6,)), dma((6,)), dma((2,)), dma((2 * LEAF,)), dma((2 * LEAF,)),
        ],
        compiler_params=pltpu.CompilerParams(collective_id=0, has_side_effects=True) if comm else None,
        name="backward",
    )(ancestors, count, own, trunk, q, do)


def local(queries, d_out, branch_latent, trunk_latent, ancestors, anc_count):
    d_queries, d_branch, d_trunk = fused_call(True, ancestors, anc_count, branch_latent, trunk_latent, queries, d_out)
    return d_queries, d_branch, d_trunk[:, None, :]


def solution(mesh):
    return jax.shard_map(
        local,
        mesh=mesh,
        in_specs=(P("leaf", "head"), P("leaf", "head"), P("leaf", None), P("leaf", None, None), P(), P()),
        out_specs=(P("leaf", "head"), P(("leaf", "head"), None), P("leaf", "head", None)),
        check_vma=False,
    )
```

```python
import functools

import jax
import jax.numpy as jnp
from jax import lax
from jax.experimental import pallas as pl
from jax.experimental.pallas import tpu as pltpu
from jax.sharding import PartitionSpec as P

F32, BF16 = jnp.float32, jnp.bfloat16
SCALE = float(192) ** -0.5
LOG2E = 1.4426950408889634
LEAF = 32
VMEM_LIMIT = 50 * 2**20
WIDE = 640


def dot(a, b, ca, cb):
    return lax.dot_general(a, b, (((ca,), (cb,)), ((), ())), preferred_element_type=F32)


def iota(shape, dim):
    return lax.broadcasted_iota(jnp.int32, shape, dim)


def listed_block(anc, leaf, branch, pick):
    rows = branch.shape[0]
    expand = (branch == iota((rows, LEAF), 1)).astype(F32).astype(BF16)
    owner = dot(expand, (anc >> 4).astype(F32).astype(BF16), 1, 0)
    local = dot(expand, (anc & 15).astype(F32).astype(BF16), 1, 0)
    mine = jnp.where(owner == leaf.astype(F32), 1.0, 0.0)
    before = jnp.where(iota((LEAF, LEAF), 0) < iota((LEAF, LEAF), 1), 1.0, 0.0).astype(BF16)
    rank = dot(mine.astype(BF16), before, 1, 0)
    chosen = jnp.where(rank == pick.astype(F32), mine, 0.0)
    return jnp.sum(chosen * (local + 1.0), axis=1, keepdims=True)


def owner_and_rank(row, slot):
    rows = slot.shape[0]
    owners = (row >> 4).astype(F32)
    at = iota((rows, LEAF), 1)
    owner = jnp.sum(jnp.where(at == slot, owners, 0.0), axis=1, keepdims=True)
    rank = jnp.sum(jnp.where((owners == owner) & (at < slot), 1.0, 0.0), axis=1, keepdims=True)
    return owner, rank


def remote(src, dst, send, recv, where):
    return pltpu.make_async_remote_copy(
        src_ref=src, dst_ref=dst, send_sem=send, recv_sem=recv, device_id=where, device_id_type=pl.DeviceIdType.MESH
    )


def signal(sem, where):
    pl.semaphore_signal(sem, inc=1, device_id=where, device_id_type=pl.DeviceIdType.MESH)


def fused(comm, anc_hbm, cnt_hbm, own_hbm, trunk_hbm, q_hbm, do_hbm, dq_ref, branch_ref, spare_ref, collect_ref,
          anc_ref, cnt_ref, own_ref, trunk_ref, small_sem,
          qs, dos, keys, sown, dpown, p_own, ds, acc_k, acc_v,
          g_out, g_got, g_tall, slabs, x_far, x_own, r_far, r_own, m_far, m_own, pair, pair_in, t_out, t_got,
          load_sem, g_send, g_recv, ring_send, ring_recv, far_send, far_recv, own_send, own_recv,
          pair_sem, t_send, t_recv):
    small = [
        pltpu.make_async_copy(anc_hbm, anc_ref, small_sem.at[0]),
        pltpu.make_async_copy(trunk_hbm, trunk_ref, small_sem.at[1]),
        pltpu.make_async_copy(own_hbm, own_ref, small_sem.at[2]),
        pltpu.make_async_copy(cnt_hbm, cnt_ref, small_sem.at[3]),
    ]
    for copy in small:
        copy.start()
    if comm:
        leaf, head = lax.axis_index("leaf"), lax.axis_index("head")
        deep, y = head // 4, lax.rem(head, 4)
        me = deep * LEAF + leaf
        right = {"head": deep * 4 + lax.rem(y + 1, 4)}
        left = {"head": deep * 4 + lax.rem(y + 3, 4)}

        def plane(p):
            return {"leaf": lax.rem(p, LEAF), "head": (p // LEAF) * 4 + y}

        barrier = pltpu.get_barrier_semaphore()

        def greet(k, c):
            signal(barrier, plane(lax.rem(me + k, 2 * LEAF)))
            return c

        lax.fori_loop(1, 2 * LEAF, greet, 0)
        signal(barrier, left)
        signal(barrier, right)
    else:
        leaf = 0

    loads = {}
    for u in range(2):
        for par in range(2):
            group = []
            for n in range(4):
                h = 4 * u + n
                at = pl.ds(192 * h, 192)
                k = 16 * u + 8 * par + 2 * n
                group.append(pltpu.make_async_copy(
                    q_hbm.at[:, pl.ds(1152 * h + 512 * par, WIDE)], qs.at[par, at], load_sem.at[k]))
                group.append(pltpu.make_async_copy(
                    do_hbm.at[:, pl.ds(1024 * h + 512 * par, 512)], dos.at[par, at], load_sem.at[k + 1]))
            for copy in group:
                copy.start()
            loads[u, par] = group
    chunks = [(u, par) for u in range(2) for par in range(2)]

    def q_of(u, par):
        return qs[par, 768 * u:768 * u + 768, :]

    def do_of(u, par):
        return dos[par, 768 * u:768 * u + 768, :]

    for copy in small:
        copy.wait()
    if comm:
        i = iota((128, 1), 0)
        block = listed_block(anc_ref[...], leaf, i // 4, (i // 2) % 2)
        want = (block - 1.0) * 8.0 + (4 * (i % 2) + y).astype(F32)
        pick = jnp.where(want == iota((128, 128), 1).astype(F32), 1.0, 0.0).astype(BF16)
        trunk = trunk_ref[...].astype(F32).reshape(128, 576).astype(BF16)
        rows = dot(pick, jnp.concatenate([trunk, jnp.zeros((128, WIDE - 576), BF16)], axis=1), 1, 0)
        for b in range(LEAF):
            g_out[b] = rows[4 * b:4 * b + 4].astype(BF16)
        i = iota((64, 1), 0)
        owner, rank = owner_and_rank(anc_ref[pl.ds(leaf, 1), :], i % 32)
        want = owner * 4.0 + rank * 2.0 + (i // 32).astype(F32)
        take = jnp.where(want == iota((64, 128), 1).astype(F32), 1.0, 0.0).astype(BF16)
        want = (i // 32).astype(F32) * 64.0 + owner * 2.0 + rank
        spread = jnp.where(want == iota((64, 128), 1).astype(F32), 1.0, 0.0).astype(BF16)
        i = iota((128, 1), 0)
        block = listed_block(anc_ref[...], leaf, (i // 2) % 32, i % 2)
        collect_ref[...] = jnp.where(block - 1.0 == iota((128, 128), 1).astype(F32), 1.0, 0.0)

    own = own_ref[...]
    blank = jnp.zeros((192, 64), BF16)
    keys[0, 0:192, :] = jnp.concatenate([own, blank], axis=1)
    keys[1, 0:192, :] = pltpu.roll(jnp.concatenate([own, blank], axis=1).astype(F32), 64, 1).astype(BF16)
    causal = jnp.where(iota((192, 192), 0) <= iota((192, 192), 1), 0.0, -1e30)

    def own_scores(c):
        for copy in loads[chunks[c]]:
            copy.wait()
        u, par = chunks[c]
        s = dot(keys[par, 0:192, :], q_of(u, par), 1, 1)
        sown[c] = s + jnp.concatenate([causal] * 4, axis=1)
        dpown[c] = dot(keys[0, 0:192, 0:512], do_of(u, par), 1, 1)

    if comm:
        pl.semaphore_wait(barrier, 2 * LEAF + 1)

        def send(k, c):
            to = lax.rem(leaf + k, LEAF)
            remote(g_out.at[to], g_got.at[leaf], g_send.at[k], g_recv.at[leaf], {"leaf": to}).start()
            return c

        lax.fori_loop(1, LEAF, send, 0)
        mine = pltpu.make_async_copy(g_out.at[leaf], g_got.at[leaf], g_recv.at[leaf])
        mine.start()
        for c in range(4):
            own_scores(c)
        mine.wait()

        def receive(k, c):
            source = lax.rem(leaf + k, LEAF)
            remote(g_out.at[source], g_got.at[source], g_send.at[k], g_recv.at[source], {"leaf": source}).wait()
            return c

        lax.fori_loop(1, LEAF, receive, 0)
        for b in range(LEAF):
            g_tall[4 * b:4 * b + 4, :] = g_got[b].astype(F32)
        slabs[y] = dot(take, g_tall[...].astype(BF16), 1, 0).astype(BF16)

        def hop(k, slab, half, where):
            part = slabs.at[slab, pl.ds(32 * half, 32)]
            return remote(part, part, ring_send.at[k], ring_recv.at[k], where)

        up, down, far = lax.rem(y + 3, 4), lax.rem(y + 1, 4), lax.rem(y + 2, 4)
        ring = [hop(0, y, 0, right), hop(1, y, 1, left), hop(2, y, 1, right), hop(3, y, 0, left)]
        for copy in ring:
            copy.start()
        hop(0, up, 0, right).wait_recv()
        ring.append(hop(4, up, 0, right))
        ring[4].start()
        hop(1, down, 1, left).wait_recv()
        ring.append(hop(5, down, 1, left))
        ring[5].start()
        hop(2, up, 1, right).wait_recv()
        hop(3, down, 0, left).wait_recv()
        hop(4, far, 0, right).wait_recv()
        hop(5, far, 1, left).wait_recv()
        for k in range(4):
            keys[0, 192 + 64 * k:256 + 64 * k, :] = slabs[lax.rem(y + k, 4)]
    else:
        for c in range(4):
            own_scores(c)
        keys[0, 192:448, :] = trunk_ref[...]
    keys[1, 192:448, :] = pltpu.roll(keys[0, 192:448, :].astype(F32), 64, 1).astype(BF16)
    live = jnp.where(iota((256, 1), 0) % 32 < cnt_ref[leaf], 0.0, -1e30)

    def far_scores(c):
        u, par = chunks[c]
        return (dot(keys[par, 192:448, :], q_of(u, par), 1, 1) + live,
                dot(keys[0, 192:448, 0:512], do_of(u, par), 1, 1))

    ahead = far_scores(0)
    for c in range(4):
        u, par = chunks[c]
        sf, dpf = ahead
        if c < 3:
            ahead = far_scores(c + 1)
        so, dpo = sown[c], dpown[c]
        m = jnp.maximum(jnp.max(sf, axis=0, keepdims=True), jnp.max(so, axis=0, keepdims=True))
        ef = jnp.exp2((sf - m) * (SCALE * LOG2E))
        eo = jnp.exp2((so - m) * (SCALE * LOG2E))
        inv = 1.0 / (jnp.sum(ef, axis=0, keepdims=True) + jnp.sum(eo, axis=0, keepdims=True))
        pf, po = ef * inv, eo * inv
        delta = jnp.sum(pf * dpf, axis=0, keepdims=True) + jnp.sum(po * dpo, axis=0, keepdims=True)
        dsf = (pf * (dpf - delta)).astype(BF16)
        ds[c, 192:448, :] = dsf
        ds[c, 0:192, :] = (po * (dpo - delta)).astype(BF16)
        p_own[c] = po.astype(BF16)
        dk = dot(dsf, q_of(u, par), 1, 0)
        dv = dot(pf.astype(BF16), do_of(u, par), 1, 0)
        if u == 0:
            acc_k[par, 192:448, :] = dk
        else:
            acc_k[par, 192:448, :] += dk
        if c == 0:
            acc_v[192:448, :] = dv
        else:
            acc_v[192:448, :] += dv

    def merged(lo, n):
        dk = (acc_k[0, lo:lo + n, :] + pltpu.roll(acc_k[1, lo:lo + n, :], 576, 1)) * SCALE
        return jnp.concatenate([dk[:, 0:512] + acc_v[lo:lo + n, :], dk[:, 512:WIDE]], axis=1)

    for k in range(4):
        for half in range(2):
            x_far[k, half] = merged(192 + 64 * k + 32 * half, 32).astype(BF16)

    def ring_start(x, mid, send_sem, recv_sem):
        copies = [
            remote(x(2, 0), mid.at[0], send_sem.at[0], recv_sem.at[0], right),
            remote(x(2, 1), mid.at[1], send_sem.at[1], recv_sem.at[1], left),
            remote(x(1, 1), mid.at[2], send_sem.at[2], recv_sem.at[2], right),
            remote(x(3, 0), mid.at[3], send_sem.at[3], recv_sem.at[3], left),
        ]
        for copy in copies:
            copy.start()
        return copies

    def ring_pass(copies, value, mid, through, send_sem, recv_sem):
        for side, k in ((0, 1), (1, 3)):
            copies[side].wait_recv()
            through[side] = (value(k, side) + mid[side].astype(F32)).astype(BF16)
            copy = remote(through.at[side], mid.at[4 + side], send_sem.at[4 + side], recv_sem.at[4 + side],
                          (right, left)[side])
            copy.start()
            copies.append(copy)

    def ring_sum(copies, value, mid):
        for k in range(2, 6):
            copies[k].wait_recv()
        return [value(0, half) + mid[4 + half].astype(F32) + mid[3 - half].astype(F32) for half in range(2)]

    if comm:
        far_copies = ring_start(lambda k, half: x_far.at[k, half], r_far, far_send, far_recv)

    def own_keys(c):
        u, par = chunks[c]
        dk = dot(ds[c, 0:192, :], q_of(u, par), 1, 0)
        dv = dot(p_own[c], do_of(u, par), 1, 0)
        if u == 0:
            acc_k[par, 0:192, :] = dk
        else:
            acc_k[par, 0:192, :] += dk
        if c == 0:
            acc_v[0:192, :] = dv
        else:
            acc_v[0:192, :] += dv

    def own_done():
        for h in range(8):
            x_own[h] = merged(24 * h, 24).astype(BF16)

    def far_value(k, half):
        return x_far[k, half].astype(F32)

    def own_at(k, half):
        return half * 4 + lax.rem(y + k, 4)

    def own_value(k, half):
        return x_own[own_at(k, half)].astype(F32)

    def d_query(u):
        even = dot(ds[2 * u], keys[0], 0, 0) * SCALE
        odd = dot(ds[2 * u + 1], keys[1], 0, 0) * SCALE
        for n in range(4):
            r = slice(192 * n, 192 * n + 192)
            at = 4608 * u + 1152 * n
            dq_ref[:, at:at + 512] = even[r, 0:512].astype(BF16)
            dq_ref[:, at + 512:at + 640] = (even[r, 512:640] + odd[r, 0:128]).astype(BF16)
            dq_ref[:, at + 640:at + 1152] = odd[r, 128:640].astype(BF16)

    if comm:
        for c in range(3):
            own_keys(c)
        ring_pass(far_copies, far_value, r_far, m_far, far_send, far_recv)
        own_keys(3)
        own_done()
        own_copies = ring_start(lambda k, half: x_own.at[own_at(k, half)], r_own, own_send, own_recv)
        sums = ring_sum(far_copies, far_value, r_far)
        rows = dot(spread, jnp.concatenate(sums, axis=0).astype(BF16), 0, 0)
        for d in range(2 * LEAF):
            t_out[d] = rows[2 * d:2 * d + 2].astype(BF16)

        def far_first(j):
            return lax.rem(j + 24, 2 * LEAF - 1) + 1

        def send_rows(j, c):
            k = far_first(j)
            to = lax.rem(me + k, 2 * LEAF)
            remote(t_out.at[to], t_got.at[me], t_send.at[k], t_recv.at[me], plane(to)).start()
            return c

        lax.fori_loop(0, 2 * LEAF - 1, send_rows, 0)
        mine = pltpu.make_async_copy(t_out.at[me], t_got.at[me], t_recv.at[me])
        mine.start()
        d_query(0)
        ring_pass(own_copies, own_value, r_own, m_own, own_send, own_recv)
        d_query(1)
        sums = ring_sum(own_copies, own_value, r_own)
        for half in range(2):
            pair[half] = sums[half]
        pair_out = remote(pair.at[1 - deep], pair_in, pair_sem.at[0], pair_sem.at[1], {"head": (1 - deep) * 4 + y})
        pair_out.start()
        mine.wait()

        def receive_rows(k, c):
            source = lax.rem(me + k, 2 * LEAF)
            remote(t_out.at[source], t_got.at[source], t_send.at[k], t_recv.at[source], plane(source)).wait()
            return c

        lax.fori_loop(1, 2 * LEAF, receive_rows, 0)
        for d in range(2 * LEAF):
            spare_ref[2 * d:2 * d + 2, :] = t_got[d].astype(F32)
        pair_out.wait()
        branch_ref[...] = pair[deep] + pair_in[...]
        for copy in ring + far_copies + own_copies:
            copy.wait_send()
    else:
        for c in range(4):
            own_keys(c)
        own_done()
        d_query(0)
        d_query(1)
        spare_ref[...] = x_far[...]
        branch_ref[...] = x_own[...]


def fused_call(comm, ancestors, count, own, trunk, q, do):
    if comm:
        small = (pltpu.VMEM((24, WIDE), F32), pltpu.VMEM((128, WIDE), F32))
    else:
        small = (pltpu.VMEM((8, 24, WIDE), BF16), pltpu.VMEM((4, 2, 32, WIDE), BF16))
    vmem, hbm = pl.BlockSpec(memory_space=pltpu.VMEM), pl.BlockSpec(memory_space=pltpu.HBM)
    dma = pltpu.SemaphoreType.DMA
    return pl.pallas_call(
        functools.partial(fused, comm),
        out_shape=(pltpu.VMEM((192, 9216), BF16),) + small + (pltpu.VMEM((128, 128), F32),),
        in_specs=[hbm] * 6,
        out_specs=(vmem,) * 4,
        scratch_shapes=[
            pltpu.VMEM((LEAF, LEAF), jnp.int32),
            pltpu.SMEM(count.shape, jnp.int32),
            pltpu.VMEM(own.shape, BF16),
            pltpu.VMEM(trunk.shape, BF16),
            dma((4,)),
            pltpu.VMEM((2, 1536, WIDE), BF16),
            pltpu.VMEM((2, 1536, 512), BF16),
            pltpu.VMEM((2, 448, WIDE), BF16),
            pltpu.VMEM((4, 192, 768), F32),
            pltpu.VMEM((4, 192, 768), F32),
            pltpu.VMEM((4, 192, 768), BF16),
            pltpu.VMEM((4, 448, 768), BF16),
            pltpu.VMEM((2, 448, WIDE), F32),
            pltpu.VMEM((448, 512), F32),
            pltpu.VMEM((LEAF, 4, WIDE), BF16),
            pltpu.VMEM((LEAF, 4, WIDE), BF16),
            pltpu.VMEM((128, WIDE), F32),
            pltpu.VMEM((4, 64, WIDE), BF16),
            pltpu.VMEM((4, 2, 32, WIDE), BF16),
            pltpu.VMEM((8, 24, WIDE), BF16),
            pltpu.VMEM((6, 32, WIDE), BF16),
            pltpu.VMEM((6, 24, WIDE), BF16),
            pltpu.VMEM((2, 32, WIDE), BF16),
            pltpu.VMEM((2, 24, WIDE), BF16),
            pltpu.VMEM((2, 24, WIDE), F32),
            pltpu.VMEM((24, WIDE), F32),
            pltpu.VMEM((2 * LEAF, 2, WIDE), BF16),
            pltpu.VMEM((2 * LEAF, 2, WIDE), BF16),
            dma((32,)), dma((LEAF,)), dma((LEAF,)), dma((6,)), dma((6,)), dma((6,)), dma((6,)),
            dma((6,)), dma((6,)), dma((2,)), dma((2 * LEAF,)), dma((2 * LEAF,)),
        ],
        compiler_params=pltpu.CompilerParams(
            collective_id=0, has_side_effects=True, vmem_limit_bytes=VMEM_LIMIT
        ) if comm else pltpu.CompilerParams(vmem_limit_bytes=VMEM_LIMIT),
        name="backward",
    )(ancestors, count, own, trunk, q, do)


def finish(grad_ref, rows_ref, sum_ref, collect_ref, dq_hbm, branch_ref, trunk_ref, sem):
    copies = []
    for k in range(4):
        part = pl.ds(48 * k, 48)
        copies.append(pltpu.make_async_copy(grad_ref.at[part], dq_hbm.at[part], sem.at[k]))
        copies[k].start()
    branch_ref[...] = sum_ref[:, 0:576]
    total = dot(collect_ref[...].astype(BF16), rows_ref[...].astype(BF16), 0, 0)
    for b in range(16):
        trunk_ref[b] = total[b:b + 1, 0:576]
    for copy in copies:
        copy.wait()


def finish_call(grad, rows, total, collect):
    vmem, hbm = pl.BlockSpec(memory_space=pltpu.VMEM), pl.BlockSpec(memory_space=pl.ANY)
    return pl.pallas_call(
        finish,
        out_shape=(
            jax.ShapeDtypeStruct((192, 9216), BF16),
            jax.ShapeDtypeStruct((24, 576), F32),
            jax.ShapeDtypeStruct((16, 1, 576), F32),
        ),
        in_specs=[vmem] * 4,
        out_specs=(hbm, vmem, vmem),
        scratch_shapes=[pltpu.SemaphoreType.DMA((4,))],
        compiler_params=pltpu.CompilerParams(vmem_limit_bytes=16 * 2**20),
        name="finish",
    )(grad, rows, total, collect)


def local(queries, d_out, branch_latent, trunk_latent, ancestors, anc_count):
    grad, total, rows, collect = fused_call(True, ancestors, anc_count, branch_latent, trunk_latent, queries, d_out)
    return finish_call(grad, rows, total, collect)


def solution(mesh):
    return jax.shard_map(
        local,
        mesh=mesh,
        in_specs=(P("leaf", "head"), P("leaf", "head"), P("leaf", None), P("leaf", None, None), P(), P()),
        out_specs=(P("leaf", "head"), P(("leaf", "head"), None), P("leaf", "head", None)),
        check_vma=False,
    )
```

```python
import functools

import jax
import jax.numpy as jnp
from jax import lax
from jax.experimental import pallas as pl
from jax.experimental.pallas import tpu as pltpu
from jax.sharding import PartitionSpec as P

F32, BF16 = jnp.float32, jnp.bfloat16
SCALE = float(192) ** -0.5
LOG2E = 1.4426950408889634
LEAF = 32
VMEM_LIMIT = 50 * 2**20
WIDE = 640


def dot(a, b, ca, cb):
    return lax.dot_general(a, b, (((ca,), (cb,)), ((), ())), preferred_element_type=F32)


def iota(shape, dim):
    return lax.broadcasted_iota(jnp.int32, shape, dim)


def listed_block(anc, leaf, branch, pick):
    rows = branch.shape[0]
    expand = (branch == iota((rows, LEAF), 1)).astype(F32).astype(BF16)
    owner = dot(expand, (anc >> 4).astype(F32).astype(BF16), 1, 0)
    local = dot(expand, (anc & 15).astype(F32).astype(BF16), 1, 0)
    mine = jnp.where(owner == leaf.astype(F32), 1.0, 0.0)
    before = jnp.where(iota((LEAF, LEAF), 0) < iota((LEAF, LEAF), 1), 1.0, 0.0).astype(BF16)
    rank = dot(mine.astype(BF16), before, 1, 0)
    chosen = jnp.where(rank == pick.astype(F32), mine, 0.0)
    return jnp.sum(chosen * (local + 1.0), axis=1, keepdims=True)


def owner_and_rank(row, slot):
    rows = slot.shape[0]
    owners = (row >> 4).astype(F32)
    at = iota((rows, LEAF), 1)
    owner = jnp.sum(jnp.where(at == slot, owners, 0.0), axis=1, keepdims=True)
    rank = jnp.sum(jnp.where((owners == owner) & (at < slot), 1.0, 0.0), axis=1, keepdims=True)
    return owner, rank


def remote(src, dst, send, recv, where):
    return pltpu.make_async_remote_copy(
        src_ref=src, dst_ref=dst, send_sem=send, recv_sem=recv, device_id=where, device_id_type=pl.DeviceIdType.MESH
    )


def signal(sem, where):
    pl.semaphore_signal(sem, inc=1, device_id=where, device_id_type=pl.DeviceIdType.MESH)


def fused(comm, anc_hbm, cnt_hbm, own_hbm, trunk_hbm, q_hbm, do_hbm, dq_ref, branch_ref, spare_ref, collect_ref,
          anc_ref, cnt_ref, own_ref, trunk_ref, small_sem,
          qs, dos, keys, sown, dpown, p_own, ds, acc_k, acc_v, dq_out,
          g_out, g_got, g_tall, slabs, x_far, x_own, r_far, r_own, m_far, m_own, pair, pair_in, t_out, t_got,
          load_sem, store_sem, g_send, g_recv, ring_send, ring_recv, far_send, far_recv, own_send, own_recv,
          pair_sem, t_send, t_recv):
    small = [
        pltpu.make_async_copy(anc_hbm, anc_ref, small_sem.at[0]),
        pltpu.make_async_copy(trunk_hbm, trunk_ref, small_sem.at[1]),
        pltpu.make_async_copy(own_hbm, own_ref, small_sem.at[2]),
        pltpu.make_async_copy(cnt_hbm, cnt_ref, small_sem.at[3]),
    ]
    for copy in small:
        copy.start()
    if comm:
        leaf, head = lax.axis_index("leaf"), lax.axis_index("head")
        deep, y = head // 4, lax.rem(head, 4)
        me = deep * LEAF + leaf
        right = {"head": deep * 4 + lax.rem(y + 1, 4)}
        left = {"head": deep * 4 + lax.rem(y + 3, 4)}

        here, there = deep * LEAF, (1 - deep) * LEAF
        across = (1 - deep) * 4 + y

        barrier = pltpu.get_barrier_semaphore()

        def greet_across(k, c):
            signal(barrier, {"leaf": k, "head": across})
            return c

        def greet(k, c):
            signal(barrier, {"leaf": lax.rem(leaf + k, LEAF)})
            return c

        lax.fori_loop(0, LEAF, greet_across, 0)
        lax.fori_loop(1, LEAF, greet, 0)
        signal(barrier, left)
        signal(barrier, right)
    else:
        leaf = 0

    loads = {}
    for u in range(2):
        for par in range(2):
            group = []
            for n in range(4):
                h = 4 * u + n
                at = pl.ds(192 * h, 192)
                k = 16 * u + 8 * par + 2 * n
                group.append(pltpu.make_async_copy(
                    q_hbm.at[:, pl.ds(1152 * h + 512 * par, WIDE)], qs.at[par, at], load_sem.at[k]))
                group.append(pltpu.make_async_copy(
                    do_hbm.at[:, pl.ds(1024 * h + 512 * par, 512)], dos.at[par, at], load_sem.at[k + 1]))
            for copy in group:
                copy.start()
            loads[u, par] = group
    chunks = [(u, par) for u in range(2) for par in range(2)]

    def q_of(u, par):
        return qs[par, 768 * u:768 * u + 768, :]

    def do_of(u, par):
        return dos[par, 768 * u:768 * u + 768, :]

    for copy in small:
        copy.wait()
    if comm:
        i = iota((128, 1), 0)
        block = listed_block(anc_ref[...], leaf, i // 4, (i // 2) % 2)
        want = (block - 1.0) * 8.0 + (4 * (i % 2) + y).astype(F32)
        pick = jnp.where(want == iota((128, 128), 1).astype(F32), 1.0, 0.0).astype(BF16)
        trunk = trunk_ref[...].astype(F32).reshape(128, 576).astype(BF16)
        rows = dot(pick, jnp.concatenate([trunk, jnp.zeros((128, WIDE - 576), BF16)], axis=1), 1, 0)
        for b in range(LEAF):
            g_out[b] = rows[4 * b:4 * b + 4].astype(BF16)

    def own_scores(c, causal):
        for copy in loads[chunks[c]]:
            copy.wait()
        u, par = chunks[c]
        s = dot(keys[par, 0:192, :], q_of(u, par), 1, 1)
        sown[c] = s + jnp.concatenate([causal] * 4, axis=1)
        dpown[c] = dot(keys[0, 0:192, 0:512], do_of(u, par), 1, 1)

    if comm:
        pl.semaphore_wait(barrier, 2 * LEAF + 1)

        def send(k, c):
            to = lax.rem(leaf + k, LEAF)
            remote(g_out.at[to], g_got.at[leaf], g_send.at[k], g_recv.at[leaf], {"leaf": to}).start()
            return c

        lax.fori_loop(1, LEAF, send, 0)
        mine = pltpu.make_async_copy(g_out.at[leaf], g_got.at[leaf], g_recv.at[leaf])
        mine.start()
        i = iota((64, 1), 0)
        owner, rank = owner_and_rank(anc_ref[pl.ds(leaf, 1), :], i % 32)
        want = owner * 4.0 + rank * 2.0 + (i // 32).astype(F32)
        take = jnp.where(want == iota((64, 128), 1).astype(F32), 1.0, 0.0).astype(BF16)
        want = (i // 32).astype(F32) * 64.0 + owner * 2.0 + rank
        spread = jnp.where(want == iota((64, 128), 1).astype(F32), 1.0, 0.0).astype(BF16)
        i = iota((128, 1), 0)
        block = listed_block(anc_ref[...], leaf, (i // 2) % 32, i % 2)
        collect_ref[...] = jnp.where(block - 1.0 == iota((128, 128), 1).astype(F32), 1.0, 0.0)
        own = own_ref[...]
        blank = jnp.zeros((192, 64), BF16)
        keys[0, 0:192, :] = jnp.concatenate([own, blank], axis=1)
        keys[1, 0:192, :] = pltpu.roll(jnp.concatenate([own, blank], axis=1).astype(F32), 64, 1).astype(BF16)
        causal = jnp.where(iota((192, 192), 0) <= iota((192, 192), 1), 0.0, -1e30)
        for c in range(4):
            own_scores(c, causal)
        mine.wait()

        def receive(k, c):
            source = lax.rem(leaf + k, LEAF)
            remote(g_out.at[source], g_got.at[source], g_send.at[k], g_recv.at[source], {"leaf": source}).wait()
            return c

        lax.fori_loop(1, LEAF, receive, 0)
        for b in range(LEAF):
            g_tall[4 * b:4 * b + 4, :] = g_got[b].astype(F32)
        slabs[y] = dot(take, g_tall[...].astype(BF16), 1, 0).astype(BF16)

        def hop(k, slab, half, where):
            part = slabs.at[slab, pl.ds(32 * half, 32)]
            return remote(part, part, ring_send.at[k], ring_recv.at[k], where)

        up, down, far = lax.rem(y + 3, 4), lax.rem(y + 1, 4), lax.rem(y + 2, 4)
        ring = [hop(0, y, 0, right), hop(1, y, 1, left), hop(2, y, 1, right), hop(3, y, 0, left)]
        for copy in ring:
            copy.start()
        hop(0, up, 0, right).wait_recv()
        ring.append(hop(4, up, 0, right))
        ring[4].start()
        hop(1, down, 1, left).wait_recv()
        ring.append(hop(5, down, 1, left))
        ring[5].start()
        hop(2, up, 1, right).wait_recv()
        hop(3, down, 0, left).wait_recv()
        hop(4, far, 0, right).wait_recv()
        hop(5, far, 1, left).wait_recv()
        for k in range(4):
            keys[0, 192 + 64 * k:256 + 64 * k, :] = slabs[lax.rem(y + k, 4)]
    else:
        own = own_ref[...]
        blank = jnp.zeros((192, 64), BF16)
        keys[0, 0:192, :] = jnp.concatenate([own, blank], axis=1)
        keys[1, 0:192, :] = pltpu.roll(jnp.concatenate([own, blank], axis=1).astype(F32), 64, 1).astype(BF16)
        causal = jnp.where(iota((192, 192), 0) <= iota((192, 192), 1), 0.0, -1e30)
        for c in range(4):
            own_scores(c, causal)
        keys[0, 192:448, :] = trunk_ref[...]
    keys[1, 192:448, :] = pltpu.roll(keys[0, 192:448, :].astype(F32), 64, 1).astype(BF16)
    live = jnp.where(iota((256, 1), 0) % 32 < cnt_ref[leaf], 0.0, -1e30)

    def far_scores(c):
        u, par = chunks[c]
        return (dot(keys[par, 192:448, :], q_of(u, par), 1, 1) + live,
                dot(keys[0, 192:448, 0:512], do_of(u, par), 1, 1))

    ahead = far_scores(0)
    for c in range(4):
        u, par = chunks[c]
        sf, dpf = ahead
        if c < 3:
            ahead = far_scores(c + 1)
        so, dpo = sown[c], dpown[c]
        m = jnp.maximum(jnp.max(sf, axis=0, keepdims=True), jnp.max(so, axis=0, keepdims=True))
        ef = jnp.exp2((sf - m) * (SCALE * LOG2E))
        eo = jnp.exp2((so - m) * (SCALE * LOG2E))
        inv = 1.0 / (jnp.sum(ef, axis=0, keepdims=True) + jnp.sum(eo, axis=0, keepdims=True))
        pf, po = ef * inv, eo * inv
        delta = jnp.sum(pf * dpf, axis=0, keepdims=True) + jnp.sum(po * dpo, axis=0, keepdims=True)
        dsf = (pf * (dpf - delta)).astype(BF16)
        ds[c, 192:448, :] = dsf
        ds[c, 0:192, :] = (po * (dpo - delta)).astype(BF16)
        p_own[c] = po.astype(BF16)
        dk = dot(dsf, q_of(u, par), 1, 0)
        dv = dot(pf.astype(BF16), do_of(u, par), 1, 0)
        if u == 0:
            acc_k[par, 192:448, :] = dk
        else:
            acc_k[par, 192:448, :] += dk
        if c == 0:
            acc_v[192:448, :] = dv
        else:
            acc_v[192:448, :] += dv

    def merged(lo, n):
        dk = (acc_k[0, lo:lo + n, :] + pltpu.roll(acc_k[1, lo:lo + n, :], 576, 1)) * SCALE
        return jnp.concatenate([dk[:, 0:512] + acc_v[lo:lo + n, :], dk[:, 512:WIDE]], axis=1)

    for k in range(4):
        for half in range(2):
            x_far[k, half] = merged(192 + 64 * k + 32 * half, 32).astype(BF16)

    def ring_start(x, mid, send_sem, recv_sem):
        copies = [
            remote(x(2, 0), mid.at[0], send_sem.at[0], recv_sem.at[0], right),
            remote(x(2, 1), mid.at[1], send_sem.at[1], recv_sem.at[1], left),
            remote(x(1, 1), mid.at[2], send_sem.at[2], recv_sem.at[2], right),
            remote(x(3, 0), mid.at[3], send_sem.at[3], recv_sem.at[3], left),
        ]
        for copy in copies:
            copy.start()
        return copies

    def ring_pass(copies, value, mid, through, send_sem, recv_sem):
        for side, k in ((0, 1), (1, 3)):
            copies[side].wait_recv()
            through[side] = (value(k, side) + mid[side].astype(F32)).astype(BF16)
            copy = remote(through.at[side], mid.at[4 + side], send_sem.at[4 + side], recv_sem.at[4 + side],
                          (right, left)[side])
            copy.start()
            copies.append(copy)

    def ring_sum(copies, value, mid):
        for k in range(2, 6):
            copies[k].wait_recv()
        return [value(0, half) + mid[4 + half].astype(F32) + mid[3 - half].astype(F32) for half in range(2)]

    if comm:
        far_copies = ring_start(lambda k, half: x_far.at[k, half], r_far, far_send, far_recv)

    def own_keys(c):
        u, par = chunks[c]
        dk = dot(ds[c, 0:192, :], q_of(u, par), 1, 0)
        dv = dot(p_own[c], do_of(u, par), 1, 0)
        if u == 0:
            acc_k[par, 0:192, :] = dk
        else:
            acc_k[par, 0:192, :] += dk
        if c == 0:
            acc_v[0:192, :] = dv
        else:
            acc_v[0:192, :] += dv

    def own_done():
        for h in range(8):
            x_own[h] = merged(24 * h, 24).astype(BF16)

    def far_value(k, half):
        return x_far[k, half].astype(F32)

    def own_at(k, half):
        return half * 4 + lax.rem(y + k, 4)

    def own_value(k, half):
        return x_own[own_at(k, half)].astype(F32)

    def d_query(u):
        even = dot(ds[2 * u], keys[0], 0, 0) * SCALE
        odd = dot(ds[2 * u + 1], keys[1], 0, 0) * SCALE
        for n in range(4):
            r = slice(192 * n, 192 * n + 192)
            at = 1152 * n
            dq_out[u, :, at:at + 512] = even[r, 0:512].astype(BF16)
            dq_out[u, :, at + 512:at + 640] = (even[r, 512:640] + odd[r, 0:128]).astype(BF16)
            dq_out[u, :, at + 640:at + 1152] = odd[r, 128:640].astype(BF16)
        copy = pltpu.make_async_copy(dq_out.at[u], dq_ref.at[:, pl.ds(4608 * u, 4608)], store_sem.at[u])
        copy.start()
        return copy

    for c in range(4):
        own_keys(c)
    own_done()
    if comm:
        ring_pass(far_copies, far_value, r_far, m_far, far_send, far_recv)
        own_copies = ring_start(lambda k, half: x_own.at[own_at(k, half)], r_own, own_send, own_recv)
        stores = [d_query(0)]
        sums = ring_sum(far_copies, far_value, r_far)
        rows = dot(spread, jnp.concatenate(sums, axis=0).astype(BF16), 0, 0)
        for d in range(2 * LEAF):
            t_out[d] = rows[2 * d:2 * d + 2].astype(BF16)

        def row_across(k):
            to = there + k
            return remote(t_out.at[to], t_got.at[me], t_send.at[k], t_recv.at[me], {"leaf": k, "head": across})

        def row_here(k):
            to = lax.rem(leaf + k, LEAF)
            return remote(t_out.at[here + to], t_got.at[me], t_send.at[LEAF + k], t_recv.at[me], {"leaf": to})

        def send_across(k, c):
            row_across(k).start()
            return c

        def send_here(k, c):
            row_here(k).start()
            return c

        lax.fori_loop(0, LEAF, send_across, 0)
        lax.fori_loop(1, LEAF, send_here, 0)
        mine = pltpu.make_async_copy(t_out.at[me], t_got.at[me], t_recv.at[me])
        mine.start()
        ring_pass(own_copies, own_value, r_own, m_own, own_send, own_recv)
        stores.append(d_query(1))
        sums = ring_sum(own_copies, own_value, r_own)
        for half in range(2):
            pair[half] = sums[half]
        pair_out = remote(pair.at[1 - deep], pair_in, pair_sem.at[0], pair_sem.at[1], {"head": across})
        pair_out.start()
        mine.wait()

        def receive_across(k, c):
            source = there + k
            row = remote(
                t_out.at[source], t_got.at[source], t_send.at[k], t_recv.at[source], {"leaf": k, "head": across}
            )
            row.wait()
            return c

        def receive_here(k, c):
            source = lax.rem(leaf + k, LEAF)
            at = here + source
            remote(t_out.at[at], t_got.at[at], t_send.at[LEAF + k], t_recv.at[at], {"leaf": source}).wait()
            return c

        lax.fori_loop(0, LEAF, receive_across, 0)
        lax.fori_loop(1, LEAF, receive_here, 0)
        for d in range(2 * LEAF):
            spare_ref[2 * d:2 * d + 2, :] = t_got[d].astype(F32)
        for copy in ring + far_copies + own_copies:
            copy.wait_send()
        for copy in stores:
            copy.wait()
        pair_out.wait()
        branch_ref[...] = pair[deep] + pair_in[...]
    else:
        stores = [d_query(0), d_query(1)]
        spare_ref[...] = x_far[...]
        branch_ref[...] = x_own[...]
        for copy in stores:
            copy.wait()


def fused_call(comm, ancestors, count, own, trunk, q, do):
    if comm:
        small = (pltpu.VMEM((24, WIDE), F32), pltpu.VMEM((128, WIDE), F32))
    else:
        small = (pltpu.VMEM((8, 24, WIDE), BF16), pltpu.VMEM((4, 2, 32, WIDE), BF16))
    vmem, hbm = pl.BlockSpec(memory_space=pltpu.VMEM), pl.BlockSpec(memory_space=pltpu.HBM)
    dma = pltpu.SemaphoreType.DMA
    return pl.pallas_call(
        functools.partial(fused, comm),
        out_shape=(pltpu.VMEM((192, 9216), BF16),) + small + (pltpu.VMEM((128, 128), F32),),
        in_specs=[hbm] * 6,
        out_specs=(pl.BlockSpec(memory_space=pl.ANY),) + (vmem,) * 3,
        scratch_shapes=[
            pltpu.VMEM((LEAF, LEAF), jnp.int32),
            pltpu.SMEM(count.shape, jnp.int32),
            pltpu.VMEM(own.shape, BF16),
            pltpu.VMEM(trunk.shape, BF16),
            dma((4,)),
            pltpu.VMEM((2, 1536, WIDE), BF16),
            pltpu.VMEM((2, 1536, 512), BF16),
            pltpu.VMEM((2, 448, WIDE), BF16),
            pltpu.VMEM((4, 192, 768), F32),
            pltpu.VMEM((4, 192, 768), F32),
            pltpu.VMEM((4, 192, 768), BF16),
            pltpu.VMEM((4, 448, 768), BF16),
            pltpu.VMEM((2, 448, WIDE), F32),
            pltpu.VMEM((448, 512), F32),
            pltpu.VMEM((2, 192, 4608), BF16),
            pltpu.VMEM((LEAF, 4, WIDE), BF16),
            pltpu.VMEM((LEAF, 4, WIDE), BF16),
            pltpu.VMEM((128, WIDE), F32),
            pltpu.VMEM((4, 64, WIDE), BF16),
            pltpu.VMEM((4, 2, 32, WIDE), BF16),
            pltpu.VMEM((8, 24, WIDE), BF16),
            pltpu.VMEM((6, 32, WIDE), BF16),
            pltpu.VMEM((6, 24, WIDE), BF16),
            pltpu.VMEM((2, 32, WIDE), BF16),
            pltpu.VMEM((2, 24, WIDE), BF16),
            pltpu.VMEM((2, 24, WIDE), F32),
            pltpu.VMEM((24, WIDE), F32),
            pltpu.VMEM((2 * LEAF, 2, WIDE), BF16),
            pltpu.VMEM((2 * LEAF, 2, WIDE), BF16),
            dma((32,)), dma((2,)), dma((LEAF,)), dma((LEAF,)), dma((6,)), dma((6,)), dma((6,)), dma((6,)),
            dma((6,)), dma((6,)), dma((2,)), dma((2 * LEAF,)), dma((2 * LEAF,)),
        ],
        compiler_params=pltpu.CompilerParams(
            collective_id=0, has_side_effects=True, vmem_limit_bytes=VMEM_LIMIT
        ) if comm else pltpu.CompilerParams(vmem_limit_bytes=VMEM_LIMIT),
        name="backward",
    )(ancestors, count, own, trunk, q, do)


def finish(grad_ref, rows_ref, sum_ref, collect_ref, dq_hbm, branch_hbm, trunk_hbm, branch, trunk, sem):
    copies = [
        pltpu.make_async_copy(grad_ref, dq_hbm, sem.at[0]),
        pltpu.make_async_copy(branch, branch_hbm, sem.at[1]),
        pltpu.make_async_copy(trunk, trunk_hbm, sem.at[2]),
    ]
    copies[0].start()
    branch[...] = sum_ref[:, 0:576]
    copies[1].start()
    total = dot(collect_ref[...].astype(BF16), rows_ref[...].astype(BF16), 0, 0)
    for b in range(16):
        trunk[b] = total[b:b + 1, 0:576]
    copies[2].start()
    for copy in copies:
        copy.wait()


def finish_call(grad, rows, total, collect):
    return pl.pallas_call(
        finish,
        out_shape=(
            jax.ShapeDtypeStruct((192, 9216), BF16),
            jax.ShapeDtypeStruct((24, 576), F32),
            jax.ShapeDtypeStruct((16, 1, 576), F32),
        ),
        in_specs=[pl.BlockSpec(memory_space=pltpu.VMEM)] * 4,
        out_specs=(pl.BlockSpec(memory_space=pltpu.HBM),) * 3,
        scratch_shapes=[
            pltpu.VMEM((24, 576), F32),
            pltpu.VMEM((16, 1, 576), F32),
            pltpu.SemaphoreType.DMA((3,)),
        ],
        compiler_params=pltpu.CompilerParams(vmem_limit_bytes=16 * 2**20),
        name="finish",
    )(grad, rows, total, collect)


def local(queries, d_out, branch_latent, trunk_latent, ancestors, anc_count):
    ancestors, anc_count = (pltpu.with_memory_space_constraint(a, pltpu.HBM) for a in (ancestors, anc_count))
    grad, total, rows, collect = fused_call(True, ancestors, anc_count, branch_latent, trunk_latent, queries, d_out)
    return finish_call(grad, rows, total, collect)


def solution(mesh):
    return jax.shard_map(
        local,
        mesh=mesh,
        in_specs=(P("leaf", "head"), P("leaf", "head"), P("leaf", None), P("leaf", None, None), P(), P()),
        out_specs=(P("leaf", "head"), P(("leaf", "head"), None), P("leaf", "head", None)),
        check_vma=False,
    )
```

```python
import functools

import jax
import jax.numpy as jnp
from jax import lax
from jax.experimental import pallas as pl
from jax.experimental.pallas import tpu as pltpu
from jax.sharding import PartitionSpec as P

F32, BF16 = jnp.float32, jnp.bfloat16
SCALE = float(192) ** -0.5
LOG2E = 1.4426950408889634
LEAF = 32
VMEM_LIMIT = 50 * 2**20
WIDE = 640


def dot(a, b, ca, cb):
    return lax.dot_general(a, b, (((ca,), (cb,)), ((), ())), preferred_element_type=F32)


def iota(shape, dim):
    return lax.broadcasted_iota(jnp.int32, shape, dim)


def listed_block(anc, leaf, branch, pick):
    rows = branch.shape[0]
    expand = (branch == iota((rows, LEAF), 1)).astype(F32).astype(BF16)
    owner = dot(expand, (anc >> 4).astype(F32).astype(BF16), 1, 0)
    local = dot(expand, (anc & 15).astype(F32).astype(BF16), 1, 0)
    mine = jnp.where(owner == leaf.astype(F32), 1.0, 0.0)
    before = jnp.where(iota((LEAF, LEAF), 0) < iota((LEAF, LEAF), 1), 1.0, 0.0).astype(BF16)
    rank = dot(mine.astype(BF16), before, 1, 0)
    chosen = jnp.where(rank == pick.astype(F32), mine, 0.0)
    return jnp.sum(chosen * (local + 1.0), axis=1, keepdims=True)


def owner_and_rank(row, slot):
    rows = slot.shape[0]
    owners = (row >> 4).astype(F32)
    at = iota((rows, LEAF), 1)
    owner = jnp.sum(jnp.where(at == slot, owners, 0.0), axis=1, keepdims=True)
    rank = jnp.sum(jnp.where((owners == owner) & (at < slot), 1.0, 0.0), axis=1, keepdims=True)
    return owner, rank


def remote(src, dst, send, recv, where):
    return pltpu.make_async_remote_copy(
        src_ref=src, dst_ref=dst, send_sem=send, recv_sem=recv, device_id=where, device_id_type=pl.DeviceIdType.MESH
    )


def signal(sem, where):
    pl.semaphore_signal(sem, inc=1, device_id=where, device_id_type=pl.DeviceIdType.MESH)


def fused(comm, anc_hbm, cnt_hbm, own_hbm, trunk_hbm, q_hbm, do_hbm, dq_ref, branch_ref, spare_ref, collect_ref,
          anc_ref, cnt_ref, own_ref, trunk_ref, small_sem,
          qs, dos, keys, sown, dpown, prob, ds, acc_k, acc_v, dq_out,
          g_out, g_got, g_tall, slabs, x_far, x_own, r_far, r_own, m_far, m_own, pair, pair_in, t_out, t_got,
          load_sem, store_sem, g_sem, ring_send, ring_recv, far_send, far_recv, own_send, own_recv,
          pair_sem, t_sem):
    small = [
        pltpu.make_async_copy(anc_hbm, anc_ref, small_sem.at[0]),
        pltpu.make_async_copy(trunk_hbm, trunk_ref, small_sem.at[1]),
        pltpu.make_async_copy(own_hbm, own_ref, small_sem.at[2]),
        pltpu.make_async_copy(cnt_hbm, cnt_ref, small_sem.at[3]),
    ]
    for copy in small:
        copy.start()
    if comm:
        leaf, head = lax.axis_index("leaf"), lax.axis_index("head")
        deep, y = head // 4, lax.rem(head, 4)
        me = deep * LEAF + leaf
        right = {"head": deep * 4 + lax.rem(y + 1, 4)}
        left = {"head": deep * 4 + lax.rem(y + 3, 4)}

        here, there = deep * LEAF, (1 - deep) * LEAF
        across = (1 - deep) * 4 + y

        barrier = pltpu.get_barrier_semaphore()

        def greet_across(k, c):
            signal(barrier, {"leaf": k, "head": across})
            return c

        def greet(k, c):
            signal(barrier, {"leaf": lax.rem(leaf + k, LEAF)})
            return c

        lax.fori_loop(0, LEAF, greet_across, 0)
        lax.fori_loop(1, LEAF, greet, 0)
        signal(barrier, left)
        signal(barrier, right)
    else:
        leaf = 0

    loads = {}
    for u in range(2):
        for par in range(2):
            k = 4 * u + 2 * par
            for n in range(4):
                h = 4 * u + n
                at = pl.ds(192 * h, 192)
                pltpu.make_async_copy(
                    q_hbm.at[:, pl.ds(1152 * h + 512 * par, WIDE)], qs.at[par, at], load_sem.at[k]).start()
                pltpu.make_async_copy(
                    do_hbm.at[:, pl.ds(1024 * h + 512 * par, 512)], dos.at[par, at], load_sem.at[k + 1]).start()
            rows = pl.ds(768 * u, 768)
            loads[u, par] = [
                pltpu.make_async_copy(ref.at[par, rows], ref.at[par, rows], load_sem.at[k + n])
                for n, ref in enumerate((qs, dos))
            ]
    chunks = [(u, par) for u in range(2) for par in range(2)]

    def q_of(u, par):
        return qs[par, 768 * u:768 * u + 768, :]

    def do_of(u, par):
        return dos[par, 768 * u:768 * u + 768, :]

    for copy in small:
        copy.wait()
    if comm:
        i = iota((128, 1), 0)
        block = listed_block(anc_ref[...], leaf, i // 4, (i // 2) % 2)
        want = (block - 1.0) * 8.0 + (4 * (i % 2) + y).astype(F32)
        pick = jnp.where(want == iota((128, 128), 1).astype(F32), 1.0, 0.0).astype(BF16)
        trunk = trunk_ref[...].astype(F32).reshape(128, 576).astype(BF16)
        rows = dot(pick, jnp.concatenate([trunk, jnp.zeros((128, WIDE - 576), BF16)], axis=1), 1, 0)
        for b in range(LEAF):
            g_out[b] = rows[4 * b:4 * b + 4].astype(BF16)

    def own_scores(c, causal):
        for copy in loads[chunks[c]]:
            copy.wait()
        u, par = chunks[c]
        s = dot(keys[par, 0:192, :], q_of(u, par), 1, 1)
        sown[c, 0:192, :] = s + jnp.concatenate([causal] * 4, axis=1)
        dpown[c, 0:192, :] = dot(keys[0, 0:192, 0:512], do_of(u, par), 1, 1)

    def live(n):
        return jnp.where(iota((n, 1), 0) % 32 < cnt_ref[leaf], 0.0, -1e30)

    def shifted(lo, hi):
        keys[1, lo:hi, :] = pltpu.roll(keys[0, lo:hi, :].astype(F32), 64, 1).astype(BF16)

    def near_scores(c):
        u, par = chunks[c]
        sown[c, 192:384, :] = dot(keys[par, 192:384, :], q_of(u, par), 1, 1) + live(192)
        dpown[c, 192:384, :] = dot(keys[0, 192:384, 0:512], do_of(u, par), 1, 1)

    if comm:
        pl.semaphore_wait(barrier, 2 * LEAF + 1)

        def send(k, c):
            to = lax.rem(leaf + k, LEAF)
            remote(g_out.at[to], g_got.at[leaf], g_sem.at[0], g_sem.at[1], {"leaf": to}).start()
            return c

        lax.fori_loop(1, LEAF, send, 0)
        mine = pltpu.make_async_copy(g_out.at[leaf], g_got.at[leaf], g_sem.at[1])
        mine.start()
        i = iota((64, 1), 0)
        owner, rank = owner_and_rank(anc_ref[pl.ds(leaf, 1), :], i % 32)
        want = owner * 4.0 + rank * 2.0 + (i // 32).astype(F32)
        take = jnp.where(want == iota((64, 128), 1).astype(F32), 1.0, 0.0).astype(BF16)
        want = (i // 32).astype(F32) * 64.0 + owner * 2.0 + rank
        spread = jnp.where(want == iota((64, 128), 1).astype(F32), 1.0, 0.0).astype(BF16)
        i = iota((128, 1), 0)
        block = listed_block(anc_ref[...], leaf, (i // 2) % 32, i % 2)
        collect_ref[...] = jnp.where(block - 1.0 == iota((128, 128), 1).astype(F32), 1.0, 0.0)
        own = own_ref[...]
        blank = jnp.zeros((192, 64), BF16)
        keys[0, 0:192, :] = jnp.concatenate([own, blank], axis=1)
        keys[1, 0:192, :] = pltpu.roll(jnp.concatenate([own, blank], axis=1).astype(F32), 64, 1).astype(BF16)
        causal = jnp.where(iota((192, 192), 0) <= iota((192, 192), 1), 0.0, -1e30)
        for c in range(4):
            own_scores(c, causal)
        others = pl.ds(0, LEAF - 1)
        remote(g_out.at[others], g_got, g_sem.at[0], g_sem.at[1], right).wait_send()
        remote(g_out, g_got, g_sem.at[0], g_sem.at[1], right).wait_recv()
        for b in range(LEAF):
            g_tall[4 * b:4 * b + 4, :] = g_got[b].astype(F32)
        slabs[y] = dot(take, g_tall[...].astype(BF16), 1, 0).astype(BF16)

        def hop(k, slab, half, where):
            part = slabs.at[slab, pl.ds(32 * half, 32)]
            return remote(part, part, ring_send.at[k], ring_recv.at[k], where)

        up, down, far = lax.rem(y + 3, 4), lax.rem(y + 1, 4), lax.rem(y + 2, 4)
        ring = [hop(0, y, 0, right), hop(1, y, 1, left), hop(2, y, 1, right), hop(3, y, 0, left)]
        for copy in ring:
            copy.start()
        hop(0, up, 0, right).wait_recv()
        ring.append(hop(4, up, 0, right))
        ring[4].start()
        hop(1, down, 1, left).wait_recv()
        ring.append(hop(5, down, 1, left))
        ring[5].start()
        hop(2, up, 1, right).wait_recv()
        hop(3, down, 0, left).wait_recv()
        for n, k in enumerate((0, 1, 3)):
            keys[0, 192 + 64 * n:256 + 64 * n, :] = slabs[lax.rem(y + k, 4)]
        shifted(192, 384)
        for c in range(4):
            near_scores(c)
        hop(4, far, 0, right).wait_recv()
        hop(5, far, 1, left).wait_recv()
        keys[0, 384:448, :] = slabs[far]
    else:
        own = own_ref[...]
        blank = jnp.zeros((192, 64), BF16)
        keys[0, 0:192, :] = jnp.concatenate([own, blank], axis=1)
        keys[1, 0:192, :] = pltpu.roll(jnp.concatenate([own, blank], axis=1).astype(F32), 64, 1).astype(BF16)
        causal = jnp.where(iota((192, 192), 0) <= iota((192, 192), 1), 0.0, -1e30)
        for c in range(4):
            own_scores(c, causal)
        keys[0, 192:320, :] = trunk_ref[0:128, :]
        keys[0, 320:384, :] = trunk_ref[192:256, :]
        shifted(192, 384)
        for c in range(4):
            near_scores(c)
        keys[0, 384:448, :] = trunk_ref[128:192, :]
    shifted(384, 448)

    def last_scores(c):
        u, par = chunks[c]
        return (dot(keys[par, 384:448, :], q_of(u, par), 1, 1) + live(64),
                dot(keys[0, 384:448, 0:512], do_of(u, par), 1, 1))

    ahead = last_scores(0)
    for c in range(4):
        u, par = chunks[c]
        sl, dpl = ahead
        if c < 3:
            ahead = last_scores(c + 1)
        so, dpo = sown[c], dpown[c]
        m = jnp.maximum(jnp.max(sl, axis=0, keepdims=True), jnp.max(so, axis=0, keepdims=True))
        el = jnp.exp2((sl - m) * (SCALE * LOG2E))
        eo = jnp.exp2((so - m) * (SCALE * LOG2E))
        inv = 1.0 / (jnp.sum(el, axis=0, keepdims=True) + jnp.sum(eo, axis=0, keepdims=True))
        pb, po = el * inv, eo * inv
        delta = jnp.sum(pb * dpl, axis=0, keepdims=True) + jnp.sum(po * dpo, axis=0, keepdims=True)
        ds[c, 0:384, :] = (po * (dpo - delta)).astype(BF16)
        ds[c, 384:448, :] = (pb * (dpl - delta)).astype(BF16)
        prob[c, 0:384, :] = po.astype(BF16)
        prob[c, 384:448, :] = pb.astype(BF16)
        dk = dot(ds[c, 192:448, :], q_of(u, par), 1, 0)
        dv = dot(prob[c, 192:448, :], do_of(u, par), 1, 0)
        if u == 0:
            acc_k[par, 192:448, :] = dk
        else:
            acc_k[par, 192:448, :] += dk
        if c == 0:
            acc_v[192:448, :] = dv
        else:
            acc_v[192:448, :] += dv

    def merged(lo, n):
        dk = (acc_k[0, lo:lo + n, :] + pltpu.roll(acc_k[1, lo:lo + n, :], 576, 1)) * SCALE
        return jnp.concatenate([dk[:, 0:512] + acc_v[lo:lo + n, :], dk[:, 512:WIDE]], axis=1)

    for at, k in enumerate((0, 1, 3, 2)):
        for half in range(2):
            x_far[k, half] = merged(192 + 64 * at + 32 * half, 32).astype(BF16)

    def ring_start(x, mid, send_sem, recv_sem):
        copies = [
            remote(x(2, 0), mid.at[0], send_sem.at[0], recv_sem.at[0], right),
            remote(x(2, 1), mid.at[1], send_sem.at[1], recv_sem.at[1], left),
            remote(x(1, 1), mid.at[2], send_sem.at[2], recv_sem.at[2], right),
            remote(x(3, 0), mid.at[3], send_sem.at[3], recv_sem.at[3], left),
        ]
        for copy in copies:
            copy.start()
        return copies

    def ring_pass(copies, value, mid, through, send_sem, recv_sem):
        for side, k in ((0, 1), (1, 3)):
            copies[side].wait_recv()
            through[side] = (value(k, side) + mid[side].astype(F32)).astype(BF16)
            copy = remote(through.at[side], mid.at[4 + side], send_sem.at[4 + side], recv_sem.at[4 + side],
                          (right, left)[side])
            copy.start()
            copies.append(copy)

    def ring_sum(copies, value, mid):
        for k in range(2, 6):
            copies[k].wait_recv()
        return [value(0, half) + mid[4 + half].astype(F32) + mid[3 - half].astype(F32) for half in range(2)]

    if comm:
        far_copies = ring_start(lambda k, half: x_far.at[k, half], r_far, far_send, far_recv)

    def own_keys(c):
        u, par = chunks[c]
        dk = dot(ds[c, 0:192, :], q_of(u, par), 1, 0)
        dv = dot(prob[c, 0:192, :], do_of(u, par), 1, 0)
        if u == 0:
            acc_k[par, 0:192, :] = dk
        else:
            acc_k[par, 0:192, :] += dk
        if c == 0:
            acc_v[0:192, :] = dv
        else:
            acc_v[0:192, :] += dv

    def own_done():
        for h in range(8):
            x_own[h] = merged(24 * h, 24).astype(BF16)

    def far_value(k, half):
        return x_far[k, half].astype(F32)

    def own_at(k, half):
        return half * 4 + lax.rem(y + k, 4)

    def own_value(k, half):
        return x_own[own_at(k, half)].astype(F32)

    def d_query(u):
        even = dot(ds[2 * u], keys[0], 0, 0) * SCALE
        odd = dot(ds[2 * u + 1], keys[1], 0, 0) * SCALE
        for n in range(4):
            r = slice(192 * n, 192 * n + 192)
            at = 1152 * n
            dq_out[u, :, at:at + 512] = even[r, 0:512].astype(BF16)
            dq_out[u, :, at + 512:at + 640] = (even[r, 512:640] + odd[r, 0:128]).astype(BF16)
            dq_out[u, :, at + 640:at + 1152] = odd[r, 128:640].astype(BF16)
        copy = pltpu.make_async_copy(dq_out.at[u], dq_ref.at[:, pl.ds(4608 * u, 4608)], store_sem.at[u])
        copy.start()
        return copy

    for c in range(4):
        own_keys(c)
    own_done()
    if comm:
        ring_pass(far_copies, far_value, r_far, m_far, far_send, far_recv)
        own_copies = ring_start(lambda k, half: x_own.at[own_at(k, half)], r_own, own_send, own_recv)
        stores = [d_query(0)]
        sums = ring_sum(far_copies, far_value, r_far)
        rows = dot(spread, jnp.concatenate(sums, axis=0).astype(BF16), 0, 0)
        ring_pass(own_copies, own_value, r_own, m_own, own_send, own_recv)
        for d in range(2 * LEAF):
            t_out[d] = rows[2 * d:2 * d + 2].astype(BF16)

        def row_across(k):
            to = there + k
            return remote(t_out.at[to], t_got.at[me], t_sem.at[0], t_sem.at[1], {"leaf": k, "head": across})

        def row_here(k):
            to = lax.rem(leaf + k, LEAF)
            return remote(t_out.at[here + to], t_got.at[me], t_sem.at[0], t_sem.at[1], {"leaf": to})

        def send_across(k, c):
            row_across(k).start()
            return c

        def send_here(k, c):
            row_here(k).start()
            return c

        lax.fori_loop(0, LEAF, send_across, 0)
        lax.fori_loop(1, LEAF, send_here, 0)
        mine = pltpu.make_async_copy(t_out.at[me], t_got.at[me], t_sem.at[1])
        mine.start()
        stores.append(d_query(1))
        sums = ring_sum(own_copies, own_value, r_own)
        for half in range(2):
            pair[half] = sums[half]
        pair_out = remote(pair.at[1 - deep], pair_in, pair_sem.at[0], pair_sem.at[1], {"head": across})
        pair_out.start()
        others = pl.ds(0, 2 * LEAF - 1)
        remote(t_out.at[others], t_got, t_sem.at[0], t_sem.at[1], right).wait_send()
        remote(t_out, t_got, t_sem.at[0], t_sem.at[1], right).wait_recv()
        for d in range(2 * LEAF):
            spare_ref[2 * d:2 * d + 2, :] = t_got[d].astype(F32)
        for copy in ring + far_copies + own_copies:
            copy.wait_send()
        for copy in stores:
            copy.wait()
        pair_out.wait()
        branch_ref[...] = pair[deep] + pair_in[...]
    else:
        stores = [d_query(0), d_query(1)]
        spare_ref[...] = x_far[...]
        branch_ref[...] = x_own[...]
        for copy in stores:
            copy.wait()


def fused_call(comm, ancestors, count, own, trunk, q, do):
    if comm:
        small = (pltpu.VMEM((24, WIDE), F32), pltpu.VMEM((128, WIDE), F32))
    else:
        small = (pltpu.VMEM((8, 24, WIDE), BF16), pltpu.VMEM((4, 2, 32, WIDE), BF16))
    vmem, hbm = pl.BlockSpec(memory_space=pltpu.VMEM), pl.BlockSpec(memory_space=pltpu.HBM)
    dma = pltpu.SemaphoreType.DMA
    return pl.pallas_call(
        functools.partial(fused, comm),
        out_shape=(pltpu.VMEM((192, 9216), BF16),) + small + (pltpu.VMEM((128, 128), F32),),
        in_specs=[hbm] * 6,
        out_specs=(pl.BlockSpec(memory_space=pl.ANY),) + (vmem,) * 3,
        scratch_shapes=[
            pltpu.VMEM((LEAF, LEAF), jnp.int32),
            pltpu.SMEM(count.shape, jnp.int32),
            pltpu.VMEM(own.shape, BF16),
            pltpu.VMEM(trunk.shape, BF16),
            dma((4,)),
            pltpu.VMEM((2, 1536, WIDE), BF16),
            pltpu.VMEM((2, 1536, 512), BF16),
            pltpu.VMEM((2, 448, WIDE), BF16),
            pltpu.VMEM((4, 384, 768), F32),
            pltpu.VMEM((4, 384, 768), F32),
            pltpu.VMEM((4, 448, 768), BF16),
            pltpu.VMEM((4, 448, 768), BF16),
            pltpu.VMEM((2, 448, WIDE), F32),
            pltpu.VMEM((448, 512), F32),
            pltpu.VMEM((2, 192, 4608), BF16),
            pltpu.VMEM((LEAF, 4, WIDE), BF16),
            pltpu.VMEM((LEAF, 4, WIDE), BF16),
            pltpu.VMEM((128, WIDE), F32),
            pltpu.VMEM((4, 64, WIDE), BF16),
            pltpu.VMEM((4, 2, 32, WIDE), BF16),
            pltpu.VMEM((8, 24, WIDE), BF16),
            pltpu.VMEM((6, 32, WIDE), BF16),
            pltpu.VMEM((6, 24, WIDE), BF16),
            pltpu.VMEM((2, 32, WIDE), BF16),
            pltpu.VMEM((2, 24, WIDE), BF16),
            pltpu.VMEM((2, 24, WIDE), F32),
            pltpu.VMEM((24, WIDE), F32),
            pltpu.VMEM((2 * LEAF, 2, WIDE), BF16),
            pltpu.VMEM((2 * LEAF, 2, WIDE), BF16),
            dma((8,)), dma((2,)), dma((2,)), dma((6,)), dma((6,)), dma((6,)), dma((6,)), dma((6,)), dma((6,)),
            dma((2,)), dma((2,)),
        ],
        compiler_params=pltpu.CompilerParams(
            collective_id=0, has_side_effects=True, vmem_limit_bytes=VMEM_LIMIT
        ) if comm else pltpu.CompilerParams(vmem_limit_bytes=VMEM_LIMIT),
        name="backward",
    )(ancestors, count, own, trunk, q, do)


def finish(grad_ref, rows_ref, sum_ref, collect_ref, dq_hbm, branch_hbm, trunk_hbm, branch, trunk, sem):
    copies = [
        pltpu.make_async_copy(grad_ref, dq_hbm, sem.at[0]),
        pltpu.make_async_copy(branch, branch_hbm, sem.at[1]),
        pltpu.make_async_copy(trunk, trunk_hbm, sem.at[2]),
    ]
    copies[0].start()
    branch[...] = sum_ref[:, 0:576]
    copies[1].start()
    total = dot(collect_ref[...].astype(BF16), rows_ref[...].astype(BF16), 0, 0)
    for b in range(16):
        trunk[b] = total[b:b + 1, 0:576]
    copies[2].start()
    for copy in copies:
        copy.wait()


def finish_call(grad, rows, total, collect):
    return pl.pallas_call(
        finish,
        out_shape=(
            jax.ShapeDtypeStruct((192, 9216), BF16),
            jax.ShapeDtypeStruct((24, 576), F32),
            jax.ShapeDtypeStruct((16, 1, 576), F32),
        ),
        in_specs=[pl.BlockSpec(memory_space=pltpu.VMEM)] * 4,
        out_specs=(pl.BlockSpec(memory_space=pltpu.HBM),) * 3,
        scratch_shapes=[
            pltpu.VMEM((24, 576), F32),
            pltpu.VMEM((16, 1, 576), F32),
            pltpu.SemaphoreType.DMA((3,)),
        ],
        compiler_params=pltpu.CompilerParams(vmem_limit_bytes=16 * 2**20),
        name="finish",
    )(grad, rows, total, collect)


def local(queries, d_out, branch_latent, trunk_latent, ancestors, anc_count):
    ancestors, anc_count = (pltpu.with_memory_space_constraint(a, pltpu.HBM) for a in (ancestors, anc_count))
    grad, total, rows, collect = fused_call(True, ancestors, anc_count, branch_latent, trunk_latent, queries, d_out)
    return finish_call(grad, rows, total, collect)


def solution(mesh):
    return jax.shard_map(
        local,
        mesh=mesh,
        in_specs=(P("leaf", "head"), P("leaf", "head"), P("leaf", None), P("leaf", None, None), P(), P()),
        out_specs=(P("leaf", "head"), P(("leaf", "head"), None), P("leaf", "head", None)),
        check_vma=False,
    )
```

```python
import functools

import jax
import jax.numpy as jnp
from jax import lax
from jax.experimental import pallas as pl
from jax.experimental.pallas import tpu as pltpu
from jax.sharding import PartitionSpec as P

F32, BF16 = jnp.float32, jnp.bfloat16
SCALE = float(192) ** -0.5
LOG2E = 1.4426950408889634
LEAF = 32
VMEM_LIMIT = 50 * 2**20
WIDE = 640


def dot(a, b, ca, cb):
    return lax.dot_general(a, b, (((ca,), (cb,)), ((), ())), preferred_element_type=F32)


def iota(shape, dim):
    return lax.broadcasted_iota(jnp.int32, shape, dim)


def listed_block(anc, leaf, branch, pick):
    rows = branch.shape[0]
    expand = (branch == iota((rows, LEAF), 1)).astype(F32).astype(BF16)
    owner = dot(expand, (anc >> 4).astype(F32).astype(BF16), 1, 0)
    local = dot(expand, (anc & 15).astype(F32).astype(BF16), 1, 0)
    mine = jnp.where(owner == leaf.astype(F32), 1.0, 0.0)
    before = jnp.where(iota((LEAF, LEAF), 0) < iota((LEAF, LEAF), 1), 1.0, 0.0).astype(BF16)
    rank = dot(mine.astype(BF16), before, 1, 0)
    chosen = jnp.where(rank == pick.astype(F32), mine, 0.0)
    return jnp.sum(chosen * (local + 1.0), axis=1, keepdims=True)


def owner_and_rank(row, slot):
    rows = slot.shape[0]
    owners = (row >> 4).astype(F32)
    at = iota((rows, LEAF), 1)
    owner = jnp.sum(jnp.where(at == slot, owners, 0.0), axis=1, keepdims=True)
    rank = jnp.sum(jnp.where((owners == owner) & (at < slot), 1.0, 0.0), axis=1, keepdims=True)
    return owner, rank


def remote(src, dst, send, recv, where):
    return pltpu.make_async_remote_copy(
        src_ref=src, dst_ref=dst, send_sem=send, recv_sem=recv, device_id=where, device_id_type=pl.DeviceIdType.MESH
    )


def signal(sem, where):
    pl.semaphore_signal(sem, inc=1, device_id=where, device_id_type=pl.DeviceIdType.MESH)


def fused(comm, anc_hbm, cnt_hbm, own_hbm, trunk_hbm, q_hbm, do_hbm, dq_ref, branch_ref, spare_ref, collect_ref,
          anc_ref, cnt_ref, own_ref, trunk_ref, small_sem,
          qs, dos, keys, eown, dpown, stats, prob, ds, acc_k, acc_v, dq_out,
          g_out, g_got, g_tall, slabs, x_far, x_own, r_far, r_own, m_far, m_own, pair, pair_in, t_out, t_got,
          load_sem, store_sem, g_sem, ring_send, ring_recv, far_send, far_recv, own_send, own_recv,
          pair_sem, t_sem):
    small = [
        pltpu.make_async_copy(anc_hbm, anc_ref, small_sem.at[0]),
        pltpu.make_async_copy(trunk_hbm, trunk_ref, small_sem.at[1]),
        pltpu.make_async_copy(own_hbm, own_ref, small_sem.at[2]),
        pltpu.make_async_copy(cnt_hbm, cnt_ref, small_sem.at[3]),
    ]
    for copy in small:
        copy.start()
    if comm:
        leaf, head = lax.axis_index("leaf"), lax.axis_index("head")
        deep, y = head // 4, lax.rem(head, 4)
        me = deep * LEAF + leaf
        right = {"head": deep * 4 + lax.rem(y + 1, 4)}
        left = {"head": deep * 4 + lax.rem(y + 3, 4)}

        z, seat = leaf // 8, lax.rem(leaf, 8)
        across = {"head": (1 - deep) * 4 + y}

        def each_seat(visit, index, where, first=0):
            def step(k, c):
                at = lax.rem(seat + k, 8) if first else k
                visit(index + at, where(at))
                return c

            lax.fori_loop(first, 8, step, 0)

        def plane_peers(visit):
            for r in (4, 3, 5, 2, 6, 1, 7, 0):
                place = lax.rem(deep * 4 + z + r, 8)
                column, base = (place // 4) * 4 + y, lax.rem(place, 4) * 8
                each_seat(visit, place * 8, lambda at: {"leaf": base + at, "head": column}, int(r == 0))

        def leaf_peers(visit):
            for other in (3 - 3 * (z // 2), 2 - z // 2, z + 1 - 2 * lax.rem(z, 2), z):
                each_seat(visit, other * 8, lambda at: {"leaf": other * 8 + at}, int(other is z))

        barrier = pltpu.get_barrier_semaphore()
        plane_peers(lambda index, where: signal(barrier, where))
        signal(barrier, left)
        signal(barrier, right)
    else:
        leaf = 0

    loads = {}
    for u in range(2):
        for par in range(2):
            k = 4 * u + 2 * par
            for n in range(4):
                h = 4 * u + n
                at = pl.ds(192 * h, 192)
                pltpu.make_async_copy(
                    q_hbm.at[:, pl.ds(1152 * h + 512 * par, WIDE)], qs.at[par, at], load_sem.at[k]).start()
                pltpu.make_async_copy(
                    do_hbm.at[:, pl.ds(1024 * h + 512 * par, 512)], dos.at[par, at], load_sem.at[k + 1]).start()
            rows = pl.ds(768 * u, 768)
            loads[u, par] = [
                pltpu.make_async_copy(ref.at[par, rows], ref.at[par, rows], load_sem.at[k + n])
                for n, ref in enumerate((qs, dos))
            ]
    chunks = [(u, par) for u in range(2) for par in range(2)]

    def q_of(u, par):
        return qs[par, 768 * u:768 * u + 768, :]

    def do_of(u, par):
        return dos[par, 768 * u:768 * u + 768, :]

    for copy in small:
        copy.wait()
    if comm:
        i = iota((128, 1), 0)
        block = listed_block(anc_ref[...], leaf, i // 4, (i // 2) % 2)
        want = (block - 1.0) * 8.0 + (4 * (i % 2) + y).astype(F32)
        pick = jnp.where(want == iota((128, 128), 1).astype(F32), 1.0, 0.0).astype(BF16)
        trunk = trunk_ref[...].astype(F32).reshape(128, 576).astype(BF16)
        rows = dot(pick, jnp.concatenate([trunk, jnp.zeros((128, WIDE - 576), BF16)], axis=1), 1, 0)
        for b in range(LEAF):
            g_out[b] = rows[4 * b:4 * b + 4].astype(BF16)

    def own_scores(c, causal):
        for copy in loads[chunks[c]]:
            copy.wait()
        u, par = chunks[c]
        s = dot(keys[par, 0:192, :], q_of(u, par), 1, 1) + jnp.concatenate([causal] * 4, axis=1)
        keep(c, 0, s, dot(keys[0, 0:192, 0:512], do_of(u, par), 1, 1))

    def keep(c, part, s, dp):
        lo, top = 192 * part, jnp.max(s, axis=0, keepdims=True)
        e = jnp.exp2((s - top) * (SCALE * LOG2E))
        eown[c, lo:lo + 192, :] = e
        dpown[c, lo:lo + 192, :] = dp
        stats[c, 3 * part:3 * part + 1, :] = top
        stats[c, 3 * part + 1:3 * part + 2, :] = jnp.sum(e, axis=0, keepdims=True)
        stats[c, 3 * part + 2:3 * part + 3, :] = jnp.sum(e * dp, axis=0, keepdims=True)

    def live(n):
        return jnp.where(iota((n, 1), 0) % 32 < cnt_ref[leaf], 0.0, -1e30)

    def shifted(lo, hi):
        keys[1, lo:hi, :] = pltpu.roll(keys[0, lo:hi, :].astype(F32), 64, 1).astype(BF16)

    def near_scores(c):
        u, par = chunks[c]
        s = dot(keys[par, 192:384, :], q_of(u, par), 1, 1) + live(192)
        keep(c, 1, s, dot(keys[0, 192:384, 0:512], do_of(u, par), 1, 1))

    if comm:
        pl.semaphore_wait(barrier, 2 * LEAF + 1)

        leaf_peers(lambda to, where: remote(g_out.at[to], g_got.at[leaf], g_sem.at[0], g_sem.at[1], where).start())
        mine = pltpu.make_async_copy(g_out.at[leaf], g_got.at[leaf], g_sem.at[1])
        mine.start()
        i = iota((64, 1), 0)
        owner, rank = owner_and_rank(anc_ref[pl.ds(leaf, 1), :], i % 32)
        want = owner * 4.0 + rank * 2.0 + (i // 32).astype(F32)
        take = jnp.where(want == iota((64, 128), 1).astype(F32), 1.0, 0.0).astype(BF16)
        want = (i // 32).astype(F32) * 64.0 + owner * 2.0 + rank
        spread = jnp.where(want == iota((64, 128), 1).astype(F32), 1.0, 0.0).astype(BF16)
        i = iota((128, 1), 0)
        block = listed_block(anc_ref[...], leaf, (i // 2) % 32, i % 2)
        collect_ref[...] = jnp.where(block - 1.0 == iota((128, 128), 1).astype(F32), 1.0, 0.0)
        own = own_ref[...]
        blank = jnp.zeros((192, 64), BF16)
        keys[0, 0:192, :] = jnp.concatenate([own, blank], axis=1)
        keys[1, 0:192, :] = pltpu.roll(jnp.concatenate([own, blank], axis=1).astype(F32), 64, 1).astype(BF16)
        causal = jnp.where(iota((192, 192), 0) <= iota((192, 192), 1), 0.0, -1e30)
        for c in range(4):
            own_scores(c, causal)
        others = pl.ds(0, LEAF - 1)
        remote(g_out.at[others], g_got, g_sem.at[0], g_sem.at[1], right).wait_send()
        remote(g_out, g_got, g_sem.at[0], g_sem.at[1], right).wait_recv()
        for b in range(LEAF):
            g_tall[4 * b:4 * b + 4, :] = g_got[b].astype(F32)
        slabs[y] = dot(take, g_tall[...].astype(BF16), 1, 0).astype(BF16)

        def hop(k, slab, half, where):
            part = slabs.at[slab, pl.ds(32 * half, 32)]
            return remote(part, part, ring_send.at[k], ring_recv.at[k], where)

        up, down, far = lax.rem(y + 3, 4), lax.rem(y + 1, 4), lax.rem(y + 2, 4)
        ring = [hop(0, y, 0, right), hop(1, y, 1, left), hop(2, y, 1, right), hop(3, y, 0, left)]
        for copy in ring:
            copy.start()
        hop(0, up, 0, right).wait_recv()
        ring.append(hop(4, up, 0, right))
        ring[4].start()
        hop(1, down, 1, left).wait_recv()
        ring.append(hop(5, down, 1, left))
        ring[5].start()
        hop(2, up, 1, right).wait_recv()
        hop(3, down, 0, left).wait_recv()
        for n, k in enumerate((0, 1, 3)):
            keys[0, 192 + 64 * n:256 + 64 * n, :] = slabs[lax.rem(y + k, 4)]
        shifted(192, 384)
        for c in range(4):
            near_scores(c)
        hop(4, far, 0, right).wait_recv()
        hop(5, far, 1, left).wait_recv()
        keys[0, 384:448, :] = slabs[far]
    else:
        own = own_ref[...]
        blank = jnp.zeros((192, 64), BF16)
        keys[0, 0:192, :] = jnp.concatenate([own, blank], axis=1)
        keys[1, 0:192, :] = pltpu.roll(jnp.concatenate([own, blank], axis=1).astype(F32), 64, 1).astype(BF16)
        causal = jnp.where(iota((192, 192), 0) <= iota((192, 192), 1), 0.0, -1e30)
        for c in range(4):
            own_scores(c, causal)
        keys[0, 192:320, :] = trunk_ref[0:128, :]
        keys[0, 320:384, :] = trunk_ref[192:256, :]
        shifted(192, 384)
        for c in range(4):
            near_scores(c)
        keys[0, 384:448, :] = trunk_ref[128:192, :]
    shifted(384, 448)

    def last_scores(c):
        u, par = chunks[c]
        return (dot(keys[par, 384:448, :], q_of(u, par), 1, 1) + live(64),
                dot(keys[0, 384:448, 0:512], do_of(u, par), 1, 1))

    ahead = last_scores(0)
    for c in range(4):
        u, par = chunks[c]
        sl, dpl = ahead
        if c < 3:
            ahead = last_scores(c + 1)
        tops = [stats[c, 3 * part:3 * part + 1, :] for part in range(2)]
        m = jnp.maximum(jnp.maximum(tops[0], tops[1]), jnp.max(sl, axis=0, keepdims=True))
        el = jnp.exp2((sl - m) * (SCALE * LOG2E))
        total, delta = jnp.sum(el, axis=0, keepdims=True), jnp.sum(el * dpl, axis=0, keepdims=True)
        factor = [jnp.exp2((top - m) * (SCALE * LOG2E)) for top in tops]
        for part in range(2):
            total = total + factor[part] * stats[c, 3 * part + 1:3 * part + 2, :]
            delta = delta + factor[part] * stats[c, 3 * part + 2:3 * part + 3, :]
        inv = 1.0 / total
        delta = delta * inv
        for part in range(2):
            rows = slice(192 * part, 192 * part + 192)
            pb = eown[c, rows, :] * (factor[part] * inv)
            prob[c, rows, :] = pb.astype(BF16)
            ds[c, rows, :] = (pb * (dpown[c, rows, :] - delta)).astype(BF16)
        pb = el * inv
        prob[c, 384:448, :] = pb.astype(BF16)
        ds[c, 384:448, :] = (pb * (dpl - delta)).astype(BF16)
        dk = dot(ds[c, 192:448, :], q_of(u, par), 1, 0)
        dv = dot(prob[c, 192:448, :], do_of(u, par), 1, 0)
        if u == 0:
            acc_k[par, 192:448, :] = dk
        else:
            acc_k[par, 192:448, :] += dk
        if c == 0:
            acc_v[192:448, :] = dv
        else:
            acc_v[192:448, :] += dv

    def merged(lo, n):
        dk = (acc_k[0, lo:lo + n, :] + pltpu.roll(acc_k[1, lo:lo + n, :], 576, 1)) * SCALE
        return jnp.concatenate([dk[:, 0:512] + acc_v[lo:lo + n, :], dk[:, 512:WIDE]], axis=1)

    for at, k in enumerate((0, 1, 3, 2)):
        for half in range(2):
            x_far[k, half] = merged(192 + 64 * at + 32 * half, 32).astype(BF16)

    def ring_start(x, mid, send_sem, recv_sem):
        copies = [
            remote(x(2, 0), mid.at[0], send_sem.at[0], recv_sem.at[0], right),
            remote(x(2, 1), mid.at[1], send_sem.at[1], recv_sem.at[1], left),
            remote(x(1, 1), mid.at[2], send_sem.at[2], recv_sem.at[2], right),
            remote(x(3, 0), mid.at[3], send_sem.at[3], recv_sem.at[3], left),
        ]
        for copy in copies:
            copy.start()
        return copies

    def ring_pass(copies, value, mid, through, send_sem, recv_sem):
        for side, k in ((0, 1), (1, 3)):
            copies[side].wait_recv()
            through[side] = (value(k, side) + mid[side].astype(F32)).astype(BF16)
            copy = remote(through.at[side], mid.at[4 + side], send_sem.at[4 + side], recv_sem.at[4 + side],
                          (right, left)[side])
            copy.start()
            copies.append(copy)

    def ring_sum(copies, value, mid):
        for k in range(2, 6):
            copies[k].wait_recv()
        return [value(0, half) + mid[4 + half].astype(F32) + mid[3 - half].astype(F32) for half in range(2)]

    if comm:
        far_copies = ring_start(lambda k, half: x_far.at[k, half], r_far, far_send, far_recv)

    def own_keys(c):
        u, par = chunks[c]
        dk = dot(ds[c, 0:192, :], q_of(u, par), 1, 0)
        dv = dot(prob[c, 0:192, :], do_of(u, par), 1, 0)
        if u == 0:
            acc_k[par, 0:192, :] = dk
        else:
            acc_k[par, 0:192, :] += dk
        if c == 0:
            acc_v[0:192, :] = dv
        else:
            acc_v[0:192, :] += dv

    def own_done():
        for h in range(8):
            x_own[h] = merged(24 * h, 24).astype(BF16)

    def far_value(k, half):
        return x_far[k, half].astype(F32)

    def own_at(k, half):
        return half * 4 + lax.rem(y + k, 4)

    def own_value(k, half):
        return x_own[own_at(k, half)].astype(F32)

    def d_query(u):
        even = dot(ds[2 * u], keys[0], 0, 0) * SCALE
        odd = dot(ds[2 * u + 1], keys[1], 0, 0) * SCALE
        for n in range(4):
            r = slice(192 * n, 192 * n + 192)
            at = 1152 * n
            dq_out[u, :, at:at + 512] = even[r, 0:512].astype(BF16)
            dq_out[u, :, at + 512:at + 640] = (even[r, 512:640] + odd[r, 0:128]).astype(BF16)
            dq_out[u, :, at + 640:at + 1152] = odd[r, 128:640].astype(BF16)
        copy = pltpu.make_async_copy(dq_out.at[u], dq_ref.at[:, pl.ds(4608 * u, 4608)], store_sem.at[u])
        copy.start()
        return copy

    for c in range(4):
        own_keys(c)
    own_done()
    if comm:
        ring_pass(far_copies, far_value, r_far, m_far, far_send, far_recv)
        own_copies = ring_start(lambda k, half: x_own.at[own_at(k, half)], r_own, own_send, own_recv)
        stores = [d_query(0)]
        sums = ring_sum(far_copies, far_value, r_far)
        rows = dot(spread, jnp.concatenate(sums, axis=0).astype(BF16), 0, 0)
        for d in range(2 * LEAF):
            t_out[d] = rows[2 * d:2 * d + 2].astype(BF16)

        plane_peers(lambda to, where: remote(t_out.at[to], t_got.at[me], t_sem.at[0], t_sem.at[1], where).start())
        mine = pltpu.make_async_copy(t_out.at[me], t_got.at[me], t_sem.at[1])
        mine.start()
        ring_pass(own_copies, own_value, r_own, m_own, own_send, own_recv)
        stores.append(d_query(1))
        sums = ring_sum(own_copies, own_value, r_own)
        for half in range(2):
            pair[half] = sums[half].astype(BF16)
        pair_out = remote(pair.at[1 - deep], pair_in, pair_sem.at[0], pair_sem.at[1], across)
        pair_out.start()
        others = pl.ds(0, 2 * LEAF - 1)
        remote(t_out.at[others], t_got, t_sem.at[0], t_sem.at[1], right).wait_send()
        remote(t_out, t_got, t_sem.at[0], t_sem.at[1], right).wait_recv()
        for d in range(2 * LEAF):
            spare_ref[2 * d:2 * d + 2, :] = t_got[d].astype(F32)
        for copy in ring + far_copies + own_copies:
            copy.wait_send()
        for copy in stores:
            copy.wait()
        pair_out.wait()
        kept = jnp.where(deep == 0, sums[0], sums[1])
        branch_ref[...] = kept + pair_in[...].astype(F32)
    else:
        stores = [d_query(0), d_query(1)]
        spare_ref[...] = x_far[...]
        branch_ref[...] = x_own[...]
        for copy in stores:
            copy.wait()


def fused_call(comm, ancestors, count, own, trunk, q, do):
    if comm:
        small = (pltpu.VMEM((24, WIDE), F32), pltpu.VMEM((128, WIDE), F32))
    else:
        small = (pltpu.VMEM((8, 24, WIDE), BF16), pltpu.VMEM((4, 2, 32, WIDE), BF16))
    vmem, hbm = pl.BlockSpec(memory_space=pltpu.VMEM), pl.BlockSpec(memory_space=pltpu.HBM)
    dma = pltpu.SemaphoreType.DMA
    return pl.pallas_call(
        functools.partial(fused, comm),
        out_shape=(pltpu.VMEM((192, 9216), BF16),) + small + (pltpu.VMEM((128, 128), F32),),
        in_specs=[hbm] * 6,
        out_specs=(pl.BlockSpec(memory_space=pl.ANY),) + (vmem,) * 3,
        scratch_shapes=[
            pltpu.VMEM((LEAF, LEAF), jnp.int32),
            pltpu.SMEM(count.shape, jnp.int32),
            pltpu.VMEM(own.shape, BF16),
            pltpu.VMEM(trunk.shape, BF16),
            dma((4,)),
            pltpu.VMEM((2, 1536, WIDE), BF16),
            pltpu.VMEM((2, 1536, 512), BF16),
            pltpu.VMEM((2, 448, WIDE), BF16),
            pltpu.VMEM((4, 384, 768), F32),
            pltpu.VMEM((4, 384, 768), F32),
            pltpu.VMEM((4, 8, 768), F32),
            pltpu.VMEM((4, 448, 768), BF16),
            pltpu.VMEM((4, 448, 768), BF16),
            pltpu.VMEM((2, 448, WIDE), F32),
            pltpu.VMEM((448, 512), F32),
            pltpu.VMEM((2, 192, 4608), BF16),
            pltpu.VMEM((LEAF, 4, WIDE), BF16),
            pltpu.VMEM((LEAF, 4, WIDE), BF16),
            pltpu.VMEM((128, WIDE), F32),
            pltpu.VMEM((4, 64, WIDE), BF16),
            pltpu.VMEM((4, 2, 32, WIDE), BF16),
            pltpu.VMEM((8, 24, WIDE), BF16),
            pltpu.VMEM((6, 32, WIDE), BF16),
            pltpu.VMEM((6, 24, WIDE), BF16),
            pltpu.VMEM((2, 32, WIDE), BF16),
            pltpu.VMEM((2, 24, WIDE), BF16),
            pltpu.VMEM((2, 24, WIDE), BF16),
            pltpu.VMEM((24, WIDE), BF16),
            pltpu.VMEM((2 * LEAF, 2, WIDE), BF16),
            pltpu.VMEM((2 * LEAF, 2, WIDE), BF16),
            dma((8,)), dma((2,)), dma((2,)), dma((6,)), dma((6,)), dma((6,)), dma((6,)), dma((6,)), dma((6,)),
            dma((2,)), dma((2,)),
        ],
        compiler_params=pltpu.CompilerParams(
            collective_id=0, has_side_effects=True, vmem_limit_bytes=VMEM_LIMIT
        ) if comm else pltpu.CompilerParams(vmem_limit_bytes=VMEM_LIMIT),
        name="backward",
    )(ancestors, count, own, trunk, q, do)


def finish(grad_ref, rows_ref, sum_ref, collect_ref, dq_hbm, branch_hbm, trunk_hbm, branch, trunk, sem):
    copies = [
        pltpu.make_async_copy(grad_ref, dq_hbm, sem.at[0]),
        pltpu.make_async_copy(branch, branch_hbm, sem.at[1]),
        pltpu.make_async_copy(trunk, trunk_hbm, sem.at[2]),
    ]
    copies[0].start()
    branch[...] = sum_ref[:, 0:576]
    copies[1].start()
    total = dot(collect_ref[...].astype(BF16), rows_ref[...].astype(BF16), 0, 0)
    for b in range(16):
        trunk[b] = total[b:b + 1, 0:576]
    copies[2].start()
    for copy in copies:
        copy.wait()


def finish_call(grad, rows, total, collect):
    return pl.pallas_call(
        finish,
        out_shape=(
            jax.ShapeDtypeStruct((192, 9216), BF16),
            jax.ShapeDtypeStruct((24, 576), F32),
            jax.ShapeDtypeStruct((16, 1, 576), F32),
        ),
        in_specs=[pl.BlockSpec(memory_space=pltpu.VMEM)] * 4,
        out_specs=(pl.BlockSpec(memory_space=pltpu.HBM),) * 3,
        scratch_shapes=[
            pltpu.VMEM((24, 576), F32),
            pltpu.VMEM((16, 1, 576), F32),
            pltpu.SemaphoreType.DMA((3,)),
        ],
        compiler_params=pltpu.CompilerParams(vmem_limit_bytes=16 * 2**20),
        name="finish",
    )(grad, rows, total, collect)


def local(queries, d_out, branch_latent, trunk_latent, ancestors, anc_count):
    ancestors, anc_count = (pltpu.with_memory_space_constraint(a, pltpu.HBM) for a in (ancestors, anc_count))
    grad, total, rows, collect = fused_call(True, ancestors, anc_count, branch_latent, trunk_latent, queries, d_out)
    return finish_call(grad, rows, total, collect)


def solution(mesh):
    return jax.shard_map(
        local,
        mesh=mesh,
        in_specs=(P("leaf", "head"), P("leaf", "head"), P("leaf", None), P("leaf", None, None), P(), P()),
        out_specs=(P("leaf", "head"), P(("leaf", "head"), None), P("leaf", "head", None)),
        check_vma=False,
    )
```

```python
import functools

import jax
import jax.numpy as jnp
from jax import lax
from jax.experimental import pallas as pl
from jax.experimental.pallas import tpu as pltpu
from jax.sharding import PartitionSpec as P

F32, BF16 = jnp.float32, jnp.bfloat16
SCALE = float(192) ** -0.5
LOG2E = 1.4426950408889634
LEAF = 32
VMEM_LIMIT = 50 * 2**20
WIDE = 640


def dot(a, b, ca, cb):
    return lax.dot_general(a, b, (((ca,), (cb,)), ((), ())), preferred_element_type=F32)


def iota(shape, dim):
    return lax.broadcasted_iota(jnp.int32, shape, dim)


def listed_block(anc, leaf, branch, pick):
    rows = branch.shape[0]
    expand = (branch == iota((rows, LEAF), 1)).astype(F32).astype(BF16)
    owner = dot(expand, (anc >> 4).astype(F32).astype(BF16), 1, 0)
    local = dot(expand, (anc & 15).astype(F32).astype(BF16), 1, 0)
    mine = jnp.where(owner == leaf.astype(F32), 1.0, 0.0)
    before = jnp.where(iota((LEAF, LEAF), 0) < iota((LEAF, LEAF), 1), 1.0, 0.0).astype(BF16)
    rank = dot(mine.astype(BF16), before, 1, 0)
    chosen = jnp.where(rank == pick.astype(F32), mine, 0.0)
    return jnp.sum(chosen * (local + 1.0), axis=1, keepdims=True)


def owner_and_rank(row, slot):
    rows = slot.shape[0]
    owners = (row >> 4).astype(F32)
    at = iota((rows, LEAF), 1)
    owner = jnp.sum(jnp.where(at == slot, owners, 0.0), axis=1, keepdims=True)
    rank = jnp.sum(jnp.where((owners == owner) & (at < slot), 1.0, 0.0), axis=1, keepdims=True)
    return owner, rank


def remote(src, dst, send, recv, where):
    return pltpu.make_async_remote_copy(
        src_ref=src, dst_ref=dst, send_sem=send, recv_sem=recv, device_id=where, device_id_type=pl.DeviceIdType.MESH
    )


def signal(sem, where):
    pl.semaphore_signal(sem, inc=1, device_id=where, device_id_type=pl.DeviceIdType.MESH)


def fused(comm, anc_hbm, cnt_hbm, own_hbm, trunk_hbm, q_hbm, do_hbm, dq_ref, branch_ref, spare_ref, collect_ref,
          anc_ref, cnt_ref, own_ref, trunk_ref, small_sem,
          qs, dos, keys, eown, dpown, stats, prob, ds, acc_k, acc_v, dq_out,
          g_out, g_got, g_tall, slabs, x_far, x_own, r_far, r_own, m_far, m_own, pair, pair_in, t_out, t_got,
          load_sem, store_sem, g_sem, ring_send, ring_recv, far_send, far_recv, own_send, own_recv,
          pair_sem, t_sem):
    small = [
        pltpu.make_async_copy(anc_hbm, anc_ref, small_sem.at[0]),
        pltpu.make_async_copy(trunk_hbm, trunk_ref, small_sem.at[1]),
        pltpu.make_async_copy(own_hbm, own_ref, small_sem.at[2]),
        pltpu.make_async_copy(cnt_hbm, cnt_ref, small_sem.at[3]),
    ]
    for copy in small:
        copy.start()
    if comm:
        leaf, head = lax.axis_index("leaf"), lax.axis_index("head")
        deep, y = head // 4, lax.rem(head, 4)
        me = deep * LEAF + leaf
        right = {"head": deep * 4 + lax.rem(y + 1, 4)}
        left = {"head": deep * 4 + lax.rem(y + 3, 4)}

        z, seat = leaf // 8, lax.rem(leaf, 8)
        across = {"head": (1 - deep) * 4 + y}

        def each_seat(visit, index, where, first=0):
            def step(k, c):
                at = lax.rem(seat + k, 8) if first else k
                visit(index + at, where(at))
                return c

            lax.fori_loop(first, 8, step, 0)

        def plane_peers(visit):
            for r in (4, 3, 5, 2, 6, 1, 7, 0):
                place = lax.rem(deep * 4 + z + r, 8)
                column, base = (place // 4) * 4 + y, lax.rem(place, 4) * 8
                each_seat(visit, place * 8, lambda at: {"leaf": base + at, "head": column}, int(r == 0))

        def leaf_peers(visit):
            for other in (3 - 3 * (z // 2), 2 - z // 2, z + 1 - 2 * lax.rem(z, 2), z):
                each_seat(visit, other * 8, lambda at: {"leaf": other * 8 + at}, int(other is z))

        barrier = pltpu.get_barrier_semaphore()
        plane_peers(lambda index, where: signal(barrier, where))
        signal(barrier, left)
        signal(barrier, right)
    else:
        leaf = 0

    loads = {}
    for u in range(2):
        for par in range(2):
            k = 4 * u + 2 * par
            for n in range(4):
                h = 4 * u + n
                at = pl.ds(192 * h, 192)
                pltpu.make_async_copy(
                    q_hbm.at[:, pl.ds(1152 * h + 512 * par, WIDE)], qs.at[par, at], load_sem.at[k]).start()
                pltpu.make_async_copy(
                    do_hbm.at[:, pl.ds(1024 * h + 512 * par, 512)], dos.at[par, at], load_sem.at[k + 1]).start()
            rows = pl.ds(768 * u, 768)
            loads[u, par] = [
                pltpu.make_async_copy(ref.at[par, rows], ref.at[par, rows], load_sem.at[k + n])
                for n, ref in enumerate((qs, dos))
            ]
    chunks = [(u, par) for u in range(2) for par in range(2)]

    def q_of(u, par):
        return qs[par, 768 * u:768 * u + 768, :]

    def do_of(u, par):
        return dos[par, 768 * u:768 * u + 768, :]

    for copy in small:
        copy.wait()
    if comm:
        i = iota((128, 1), 0)
        block = listed_block(anc_ref[...], leaf, i // 4, (i // 2) % 2)
        want = (block - 1.0) * 8.0 + (4 * (i % 2) + y).astype(F32)
        pick = jnp.where(want == iota((128, 128), 1).astype(F32), 1.0, 0.0).astype(BF16)
        trunk = trunk_ref[...].astype(F32).reshape(128, 576).astype(BF16)
        rows = dot(pick, jnp.concatenate([trunk, jnp.zeros((128, WIDE - 576), BF16)], axis=1), 1, 0)
        for b in range(LEAF):
            g_out[b] = rows[4 * b:4 * b + 4].astype(BF16)

    def own_scores(c, causal):
        for copy in loads[chunks[c]]:
            copy.wait()
        u, par = chunks[c]
        s = dot(keys[par, 0:192, :], q_of(u, par), 1, 1) + jnp.concatenate([causal] * 4, axis=1)
        keep(c, 0, s, dot(keys[0, 0:192, 0:512], do_of(u, par), 1, 1))

    def keep(c, part, s, dp):
        lo, top = 192 * part, jnp.max(s, axis=0, keepdims=True)
        e = jnp.exp2((s - top) * (SCALE * LOG2E))
        eown[c, lo:lo + 192, :] = e
        dpown[c, lo:lo + 192, :] = dp
        stats[c, 3 * part:3 * part + 1, :] = top
        stats[c, 3 * part + 1:3 * part + 2, :] = jnp.sum(e, axis=0, keepdims=True)
        stats[c, 3 * part + 2:3 * part + 3, :] = jnp.sum(e * dp, axis=0, keepdims=True)

    def live(n):
        return jnp.where(iota((n, 1), 0) % 32 < cnt_ref[leaf], 0.0, -1e30)

    def shifted(lo, hi):
        keys[1, lo:hi, :] = pltpu.roll(keys[0, lo:hi, :].astype(F32), 64, 1).astype(BF16)

    def near_scores(c):
        u, par = chunks[c]
        s = dot(keys[par, 192:384, :], q_of(u, par), 1, 1) + live(192)
        keep(c, 1, s, dot(keys[0, 192:384, 0:512], do_of(u, par), 1, 1))

    if comm:
        pl.semaphore_wait(barrier, 2 * LEAF + 1)

        leaf_peers(lambda to, where: remote(g_out.at[to], g_got.at[leaf], g_sem.at[0], g_sem.at[1], where).start())
        mine = pltpu.make_async_copy(g_out.at[leaf], g_got.at[leaf], g_sem.at[1])
        mine.start()
        i = iota((64, 1), 0)
        owner, rank = owner_and_rank(anc_ref[pl.ds(leaf, 1), :], i % 32)
        want = owner * 4.0 + rank * 2.0 + (i // 32).astype(F32)
        take = jnp.where(want == iota((64, 128), 1).astype(F32), 1.0, 0.0).astype(BF16)
        want = (i // 32).astype(F32) * 64.0 + owner * 2.0 + rank
        spread = jnp.where(want == iota((64, 128), 1).astype(F32), 1.0, 0.0).astype(BF16)
        i = iota((128, 1), 0)
        block = listed_block(anc_ref[...], leaf, (i // 2) % 32, i % 2)
        collect_ref[...] = jnp.where(block - 1.0 == iota((128, 128), 1).astype(F32), 1.0, 0.0)
        own = own_ref[...]
        blank = jnp.zeros((192, 64), BF16)
        keys[0, 0:192, :] = jnp.concatenate([own, blank], axis=1)
        keys[1, 0:192, :] = pltpu.roll(jnp.concatenate([own, blank], axis=1).astype(F32), 64, 1).astype(BF16)
        causal = jnp.where(iota((192, 192), 0) <= iota((192, 192), 1), 0.0, -1e30)
        for c in range(4):
            own_scores(c, causal)
        others = pl.ds(0, LEAF - 1)
        remote(g_out.at[others], g_got, g_sem.at[0], g_sem.at[1], right).wait_send()
        remote(g_out, g_got, g_sem.at[0], g_sem.at[1], right).wait_recv()
        for b in range(LEAF):
            g_tall[4 * b:4 * b + 4, :] = g_got[b].astype(F32)
        slabs[y] = dot(take, g_tall[...].astype(BF16), 1, 0).astype(BF16)

        def hop(k, slab, half, where):
            part = slabs.at[slab, pl.ds(32 * half, 32)]
            return remote(part, part, ring_send.at[k], ring_recv.at[k], where)

        up, down, far = lax.rem(y + 3, 4), lax.rem(y + 1, 4), lax.rem(y + 2, 4)
        ring = [hop(0, y, 0, right), hop(1, y, 1, left), hop(2, y, 1, right), hop(3, y, 0, left)]
        for copy in ring:
            copy.start()
        hop(0, up, 0, right).wait_recv()
        ring.append(hop(4, up, 0, right))
        ring[4].start()
        hop(1, down, 1, left).wait_recv()
        ring.append(hop(5, down, 1, left))
        ring[5].start()
        hop(2, up, 1, right).wait_recv()
        hop(3, down, 0, left).wait_recv()
        for n, k in enumerate((0, 1, 3)):
            keys[0, 192 + 64 * n:256 + 64 * n, :] = slabs[lax.rem(y + k, 4)]
        shifted(192, 384)
        for c in range(4):
            near_scores(c)
        hop(4, far, 0, right).wait_recv()
        hop(5, far, 1, left).wait_recv()
        keys[0, 384:448, :] = slabs[far]
    else:
        own = own_ref[...]
        blank = jnp.zeros((192, 64), BF16)
        keys[0, 0:192, :] = jnp.concatenate([own, blank], axis=1)
        keys[1, 0:192, :] = pltpu.roll(jnp.concatenate([own, blank], axis=1).astype(F32), 64, 1).astype(BF16)
        causal = jnp.where(iota((192, 192), 0) <= iota((192, 192), 1), 0.0, -1e30)
        for c in range(4):
            own_scores(c, causal)
        keys[0, 192:320, :] = trunk_ref[0:128, :]
        keys[0, 320:384, :] = trunk_ref[192:256, :]
        shifted(192, 384)
        for c in range(4):
            near_scores(c)
        keys[0, 384:448, :] = trunk_ref[128:192, :]
    shifted(384, 448)

    def last_scores(c):
        u, par = chunks[c]
        return (dot(keys[par, 384:448, :], q_of(u, par), 1, 1) + live(64),
                dot(keys[0, 384:448, 0:512], do_of(u, par), 1, 1))

    ahead = last_scores(0)
    for c in range(4):
        u, par = chunks[c]
        sl, dpl = ahead
        if c < 3:
            ahead = last_scores(c + 1)
        tops = [stats[c, 3 * part:3 * part + 1, :] for part in range(2)]
        m = jnp.maximum(jnp.maximum(tops[0], tops[1]), jnp.max(sl, axis=0, keepdims=True))
        el = jnp.exp2((sl - m) * (SCALE * LOG2E))
        total, delta = jnp.sum(el, axis=0, keepdims=True), jnp.sum(el * dpl, axis=0, keepdims=True)
        factor = [jnp.exp2((top - m) * (SCALE * LOG2E)) for top in tops]
        for part in range(2):
            total = total + factor[part] * stats[c, 3 * part + 1:3 * part + 2, :]
            delta = delta + factor[part] * stats[c, 3 * part + 2:3 * part + 3, :]
        inv = 1.0 / total
        delta = delta * inv
        for part in range(2):
            rows = slice(192 * part, 192 * part + 192)
            pb = eown[c, rows, :] * (factor[part] * inv)
            prob[c, rows, :] = pb.astype(BF16)
            ds[c, rows, :] = (pb * (dpown[c, rows, :] - delta)).astype(BF16)
        pb = el * inv
        prob[c, 384:448, :] = pb.astype(BF16)
        ds[c, 384:448, :] = (pb * (dpl - delta)).astype(BF16)
        dk = dot(ds[c, 192:448, :], q_of(u, par), 1, 0)
        dv = dot(prob[c, 192:448, :], do_of(u, par), 1, 0)
        if u == 0:
            acc_k[par, 192:448, :] = dk
        else:
            acc_k[par, 192:448, :] += dk
        if c == 0:
            acc_v[192:448, :] = dv
        else:
            acc_v[192:448, :] += dv

    def merged(lo, n):
        dk = (acc_k[0, lo:lo + n, :] + pltpu.roll(acc_k[1, lo:lo + n, :], 576, 1)) * SCALE
        return jnp.concatenate([dk[:, 0:512] + acc_v[lo:lo + n, :], dk[:, 512:WIDE]], axis=1)

    for at, k in enumerate((0, 1, 3, 2)):
        for half in range(2):
            x_far[k, half] = merged(192 + 64 * at + 32 * half, 32).astype(BF16)

    def ring_start(x, mid, send_sem, recv_sem):
        copies = [
            remote(x(2, 0), mid.at[0], send_sem.at[0], recv_sem.at[0], right),
            remote(x(2, 1), mid.at[1], send_sem.at[1], recv_sem.at[1], left),
            remote(x(1, 1), mid.at[2], send_sem.at[2], recv_sem.at[2], right),
            remote(x(3, 0), mid.at[3], send_sem.at[3], recv_sem.at[3], left),
        ]
        for copy in copies:
            copy.start()
        return copies

    def ring_pass(copies, value, mid, through, send_sem, recv_sem):
        for side, k in ((0, 1), (1, 3)):
            copies[side].wait_recv()
            through[side] = (value(k, side) + mid[side].astype(F32)).astype(BF16)
            copy = remote(through.at[side], mid.at[4 + side], send_sem.at[4 + side], recv_sem.at[4 + side],
                          (right, left)[side])
            copy.start()
            copies.append(copy)

    def ring_sum(copies, value, mid):
        for k in range(2, 6):
            copies[k].wait_recv()
        return [value(0, half) + mid[4 + half].astype(F32) + mid[3 - half].astype(F32) for half in range(2)]

    if comm:
        far_copies = ring_start(lambda k, half: x_far.at[k, half], r_far, far_send, far_recv)

    def own_keys(c):
        u, par = chunks[c]
        dk = dot(ds[c, 0:192, :], q_of(u, par), 1, 0)
        dv = dot(prob[c, 0:192, :], do_of(u, par), 1, 0)
        if u == 0:
            acc_k[par, 0:192, :] = dk
        else:
            acc_k[par, 0:192, :] += dk
        if c == 0:
            acc_v[0:192, :] = dv
        else:
            acc_v[0:192, :] += dv

    def own_done():
        for h in range(8):
            x_own[h] = merged(24 * h, 24).astype(BF16)

    def far_value(k, half):
        return x_far[k, half].astype(F32)

    def own_at(k, half):
        return half * 4 + lax.rem(y + k, 4)

    def own_value(k, half):
        return x_own[own_at(k, half)].astype(F32)

    def d_query(u):
        even = dot(ds[2 * u], keys[0], 0, 0) * SCALE
        odd = dot(ds[2 * u + 1], keys[1], 0, 0) * SCALE
        for n in range(4):
            r = slice(192 * n, 192 * n + 192)
            at = 1152 * n
            dq_out[u, :, at:at + 512] = even[r, 0:512].astype(BF16)
            dq_out[u, :, at + 512:at + 640] = (even[r, 512:640] + odd[r, 0:128]).astype(BF16)
            dq_out[u, :, at + 640:at + 1152] = odd[r, 128:640].astype(BF16)
        copy = pltpu.make_async_copy(dq_out.at[u], dq_ref.at[:, pl.ds(4608 * u, 4608)], store_sem.at[u])
        copy.start()
        return copy

    for c in range(4):
        own_keys(c)
    own_done()
    if comm:
        own_copies = ring_start(lambda k, half: x_own.at[own_at(k, half)], r_own, own_send, own_recv)
        ring_pass(far_copies, far_value, r_far, m_far, far_send, far_recv)
        stores = [d_query(0)]
        ring_pass(own_copies, own_value, r_own, m_own, own_send, own_recv)
        sums = ring_sum(far_copies, far_value, r_far)
        rows = dot(spread, jnp.concatenate(sums, axis=0).astype(BF16), 0, 0)
        for d in range(2 * LEAF):
            t_out[d] = rows[2 * d:2 * d + 2].astype(BF16)

        plane_peers(lambda to, where: remote(t_out.at[to], t_got.at[me], t_sem.at[0], t_sem.at[1], where).start())
        mine = pltpu.make_async_copy(t_out.at[me], t_got.at[me], t_sem.at[1])
        mine.start()
        sums = ring_sum(own_copies, own_value, r_own)
        for half in range(2):
            pair[half] = sums[half].astype(BF16)
        pair_out = remote(pair.at[1 - deep], pair_in, pair_sem.at[0], pair_sem.at[1], across)
        pair_out.start()
        stores.append(d_query(1))
        others = pl.ds(0, 2 * LEAF - 1)
        remote(t_out.at[others], t_got, t_sem.at[0], t_sem.at[1], right).wait_send()
        remote(t_out, t_got, t_sem.at[0], t_sem.at[1], right).wait_recv()
        for d in range(2 * LEAF):
            spare_ref[2 * d:2 * d + 2, :] = t_got[d].astype(F32)
        for copy in ring + far_copies + own_copies:
            copy.wait_send()
        for copy in stores:
            copy.wait()
        pair_out.wait()
        kept = jnp.where(deep == 0, sums[0], sums[1])
        branch_ref[...] = kept + pair_in[...].astype(F32)
    else:
        stores = [d_query(0), d_query(1)]
        spare_ref[...] = x_far[...]
        branch_ref[...] = x_own[...]
        for copy in stores:
            copy.wait()


def fused_call(comm, ancestors, count, own, trunk, q, do):
    if comm:
        small = (pltpu.VMEM((24, WIDE), F32), pltpu.VMEM((128, WIDE), F32))
    else:
        small = (pltpu.VMEM((8, 24, WIDE), BF16), pltpu.VMEM((4, 2, 32, WIDE), BF16))
    vmem, hbm = pl.BlockSpec(memory_space=pltpu.VMEM), pl.BlockSpec(memory_space=pltpu.HBM)
    dma = pltpu.SemaphoreType.DMA
    return pl.pallas_call(
        functools.partial(fused, comm),
        out_shape=(pltpu.VMEM((192, 9216), BF16),) + small + (pltpu.VMEM((128, 128), F32),),
        in_specs=[hbm] * 6,
        out_specs=(pl.BlockSpec(memory_space=pl.ANY),) + (vmem,) * 3,
        scratch_shapes=[
            pltpu.VMEM((LEAF, LEAF), jnp.int32),
            pltpu.SMEM(count.shape, jnp.int32),
            pltpu.VMEM(own.shape, BF16),
            pltpu.VMEM(trunk.shape, BF16),
            dma((4,)),
            pltpu.VMEM((2, 1536, WIDE), BF16),
            pltpu.VMEM((2, 1536, 512), BF16),
            pltpu.VMEM((2, 448, WIDE), BF16),
            pltpu.VMEM((4, 384, 768), F32),
            pltpu.VMEM((4, 384, 768), F32),
            pltpu.VMEM((4, 8, 768), F32),
            pltpu.VMEM((4, 448, 768), BF16),
            pltpu.VMEM((4, 448, 768), BF16),
            pltpu.VMEM((2, 448, WIDE), F32),
            pltpu.VMEM((448, 512), F32),
            pltpu.VMEM((2, 192, 4608), BF16),
            pltpu.VMEM((LEAF, 4, WIDE), BF16),
            pltpu.VMEM((LEAF, 4, WIDE), BF16),
            pltpu.VMEM((128, WIDE), F32),
            pltpu.VMEM((4, 64, WIDE), BF16),
            pltpu.VMEM((4, 2, 32, WIDE), BF16),
            pltpu.VMEM((8, 24, WIDE), BF16),
            pltpu.VMEM((6, 32, WIDE), BF16),
            pltpu.VMEM((6, 24, WIDE), BF16),
            pltpu.VMEM((2, 32, WIDE), BF16),
            pltpu.VMEM((2, 24, WIDE), BF16),
            pltpu.VMEM((2, 24, WIDE), BF16),
            pltpu.VMEM((24, WIDE), BF16),
            pltpu.VMEM((2 * LEAF, 2, WIDE), BF16),
            pltpu.VMEM((2 * LEAF, 2, WIDE), BF16),
            dma((8,)), dma((2,)), dma((2,)), dma((6,)), dma((6,)), dma((6,)), dma((6,)), dma((6,)), dma((6,)),
            dma((2,)), dma((2,)),
        ],
        compiler_params=pltpu.CompilerParams(
            collective_id=0, has_side_effects=True, vmem_limit_bytes=VMEM_LIMIT
        ) if comm else pltpu.CompilerParams(vmem_limit_bytes=VMEM_LIMIT),
        name="backward",
    )(ancestors, count, own, trunk, q, do)


def finish(grad_ref, rows_ref, sum_ref, collect_ref, dq_hbm, branch_hbm, trunk_hbm, branch, trunk, sem):
    copies = [
        pltpu.make_async_copy(grad_ref, dq_hbm, sem.at[0]),
        pltpu.make_async_copy(branch, branch_hbm, sem.at[1]),
        pltpu.make_async_copy(trunk, trunk_hbm, sem.at[2]),
    ]
    copies[0].start()
    branch[...] = sum_ref[:, 0:576]
    copies[1].start()
    total = dot(collect_ref[...].astype(BF16), rows_ref[...].astype(BF16), 0, 0)
    for b in range(16):
        trunk[b] = total[b:b + 1, 0:576]
    copies[2].start()
    for copy in copies:
        copy.wait()


def finish_call(grad, rows, total, collect):
    return pl.pallas_call(
        finish,
        out_shape=(
            jax.ShapeDtypeStruct((192, 9216), BF16),
            jax.ShapeDtypeStruct((24, 576), F32),
            jax.ShapeDtypeStruct((16, 1, 576), F32),
        ),
        in_specs=[pl.BlockSpec(memory_space=pltpu.VMEM)] * 4,
        out_specs=(pl.BlockSpec(memory_space=pltpu.HBM),) * 3,
        scratch_shapes=[
            pltpu.VMEM((24, 576), F32),
            pltpu.VMEM((16, 1, 576), F32),
            pltpu.SemaphoreType.DMA((3,)),
        ],
        compiler_params=pltpu.CompilerParams(vmem_limit_bytes=16 * 2**20),
        name="finish",
    )(grad, rows, total, collect)


def local(queries, d_out, branch_latent, trunk_latent, ancestors, anc_count):
    ancestors, anc_count = (pltpu.with_memory_space_constraint(a, pltpu.HBM) for a in (ancestors, anc_count))
    grad, total, rows, collect = fused_call(True, ancestors, anc_count, branch_latent, trunk_latent, queries, d_out)
    return finish_call(grad, rows, total, collect)


def solution(mesh):
    return jax.shard_map(
        local,
        mesh=mesh,
        in_specs=(P("leaf", "head"), P("leaf", "head"), P("leaf", None), P("leaf", None, None), P(), P()),
        out_specs=(P("leaf", "head"), P(("leaf", "head"), None), P("leaf", "head", None)),
        check_vma=False,
    )
```

```python
import functools

import jax
import jax.numpy as jnp
from jax import lax
from jax.experimental import pallas as pl
from jax.experimental.pallas import tpu as pltpu
from jax.sharding import PartitionSpec as P

F32, BF16 = jnp.float32, jnp.bfloat16
SCALE = float(192) ** -0.5
LOG2E = 1.4426950408889634
LEAF = 32
VMEM_LIMIT = 50 * 2**20
WIDE = 640


def dot(a, b, ca, cb):
    return lax.dot_general(a, b, (((ca,), (cb,)), ((), ())), preferred_element_type=F32)


def iota(shape, dim):
    return lax.broadcasted_iota(jnp.int32, shape, dim)


def listed_block(anc, leaf, branch, pick):
    rows = branch.shape[0]
    expand = (branch == iota((rows, LEAF), 1)).astype(F32).astype(BF16)
    owner = dot(expand, (anc >> 4).astype(F32).astype(BF16), 1, 0)
    local = dot(expand, (anc & 15).astype(F32).astype(BF16), 1, 0)
    mine = jnp.where(owner == leaf.astype(F32), 1.0, 0.0)
    before = jnp.where(iota((LEAF, LEAF), 0) < iota((LEAF, LEAF), 1), 1.0, 0.0).astype(BF16)
    rank = dot(mine.astype(BF16), before, 1, 0)
    chosen = jnp.where(rank == pick.astype(F32), mine, 0.0)
    return jnp.sum(chosen * (local + 1.0), axis=1, keepdims=True)


def owner_and_rank(row, slot):
    rows = slot.shape[0]
    owners = (row >> 4).astype(F32)
    at = iota((rows, LEAF), 1)
    owner = jnp.sum(jnp.where(at == slot, owners, 0.0), axis=1, keepdims=True)
    rank = jnp.sum(jnp.where((owners == owner) & (at < slot), 1.0, 0.0), axis=1, keepdims=True)
    return owner, rank


def remote(src, dst, send, recv, where):
    return pltpu.make_async_remote_copy(
        src_ref=src, dst_ref=dst, send_sem=send, recv_sem=recv, device_id=where, device_id_type=pl.DeviceIdType.MESH
    )


def signal(sem, where):
    pl.semaphore_signal(sem, inc=1, device_id=where, device_id_type=pl.DeviceIdType.MESH)


def fused(comm, anc_hbm, cnt_hbm, own_hbm, trunk_hbm, q_hbm, do_hbm, dq_ref, branch_ref, spare_ref, collect_ref,
          anc_ref, cnt_ref, own_ref, trunk_ref, small_sem,
          qs, dos, keys, eown, dpown, stats, prob, ds, acc_k, acc_v, dq_out,
          g_out, g_got, g_tall, slabs, x_far, x_own, r_far, r_own, m_far, m_own, pair, pair_in, t_out, t_got,
          load_sem, store_sem, g_sem, ring_send, ring_recv, far_send, far_recv, own_send, own_recv,
          pair_sem, t_sem):
    small = [
        pltpu.make_async_copy(anc_hbm, anc_ref, small_sem.at[0]),
        pltpu.make_async_copy(trunk_hbm, trunk_ref, small_sem.at[1]),
        pltpu.make_async_copy(own_hbm, own_ref, small_sem.at[2]),
        pltpu.make_async_copy(cnt_hbm, cnt_ref, small_sem.at[3]),
    ]
    for copy in small:
        copy.start()
    if comm:
        leaf, head = lax.axis_index("leaf"), lax.axis_index("head")
        deep, y = head // 4, lax.rem(head, 4)
        me = deep * LEAF + leaf
        right = {"head": deep * 4 + lax.rem(y + 1, 4)}
        left = {"head": deep * 4 + lax.rem(y + 3, 4)}

        z, seat = leaf // 8, lax.rem(leaf, 8)
        across = {"head": (1 - deep) * 4 + y}

        def each_seat(visit, index, where, first=0):
            def step(k, c):
                at = lax.rem(seat + k, 8) if first else k
                visit(index + at, where(at))
                return c

            lax.fori_loop(first, 8, step, 0)

        def plane_peers(visit):
            for r in (4, 3, 5, 2, 6, 1, 7, 0):
                place = lax.rem(deep * 4 + z + r, 8)
                column, base = (place // 4) * 4 + y, lax.rem(place, 4) * 8
                each_seat(visit, place * 8, lambda at: {"leaf": base + at, "head": column}, int(r == 0))

        def leaf_peers(visit):
            for other in (3 - 3 * (z // 2), 2 - z // 2, z + 1 - 2 * lax.rem(z, 2), z):
                each_seat(visit, other * 8, lambda at: {"leaf": other * 8 + at}, int(other is z))

        barrier = pltpu.get_barrier_semaphore()
        plane_peers(lambda index, where: signal(barrier, where))
        signal(barrier, left)
        signal(barrier, right)
    else:
        leaf = 0

    loads = {}
    for u in range(2):
        for par in range(2):
            k = 4 * u + 2 * par
            for n in range(4):
                h = 4 * u + n
                at = pl.ds(192 * h, 192)
                pltpu.make_async_copy(
                    q_hbm.at[:, pl.ds(1152 * h + 512 * par, WIDE)], qs.at[par, at], load_sem.at[k]).start()
                pltpu.make_async_copy(
                    do_hbm.at[:, pl.ds(1024 * h + 512 * par, 512)], dos.at[par, at], load_sem.at[k + 1]).start()
            rows = pl.ds(768 * u, 768)
            loads[u, par] = [
                pltpu.make_async_copy(ref.at[par, rows], ref.at[par, rows], load_sem.at[k + n])
                for n, ref in enumerate((qs, dos))
            ]
    chunks = [(u, par) for u in range(2) for par in range(2)]

    def q_of(u, par):
        return qs[par, 768 * u:768 * u + 768, :]

    def do_of(u, par):
        return dos[par, 768 * u:768 * u + 768, :]

    for copy in small:
        copy.wait()
    if comm:
        i = iota((128, 1), 0)
        block = listed_block(anc_ref[...], leaf, i // 4, (i // 2) % 2)
        want = (block - 1.0) * 8.0 + (4 * (i % 2) + y).astype(F32)
        pick = jnp.where(want == iota((128, 128), 1).astype(F32), 1.0, 0.0).astype(BF16)
        trunk = trunk_ref[...].astype(F32).reshape(128, 576).astype(BF16)
        rows = dot(pick, jnp.concatenate([trunk, jnp.zeros((128, WIDE - 576), BF16)], axis=1), 1, 0)
        for b in range(LEAF):
            g_out[b] = rows[4 * b:4 * b + 4].astype(BF16)

    def own_scores(c, causal):
        for copy in loads[chunks[c]]:
            copy.wait()
        u, par = chunks[c]
        s = dot(keys[par, 0:192, :], q_of(u, par), 1, 1) + jnp.concatenate([causal] * 4, axis=1)
        keep(c, 0, s, dot(keys[0, 0:192, 0:512], do_of(u, par), 1, 1))

    def keep(c, part, s, dp):
        lo, top = 192 * part, jnp.max(s, axis=0, keepdims=True)
        e = jnp.exp2((s - top) * (SCALE * LOG2E))
        eown[c, lo:lo + 192, :] = e
        dpown[c, lo:lo + 192, :] = dp
        stats[c, 3 * part:3 * part + 1, :] = top
        stats[c, 3 * part + 1:3 * part + 2, :] = jnp.sum(e, axis=0, keepdims=True)
        stats[c, 3 * part + 2:3 * part + 3, :] = jnp.sum(e * dp, axis=0, keepdims=True)

    def live(n):
        return jnp.where(iota((n, 1), 0) % 32 < cnt_ref[leaf], 0.0, -1e30)

    def shifted(lo, hi):
        keys[1, lo:hi, :] = pltpu.roll(keys[0, lo:hi, :].astype(F32), 64, 1).astype(BF16)

    def near_scores(c):
        u, par = chunks[c]
        s = dot(keys[par, 192:384, :], q_of(u, par), 1, 1) + live(192)
        keep(c, 1, s, dot(keys[0, 192:384, 0:512], do_of(u, par), 1, 1))

    if comm:
        pl.semaphore_wait(barrier, 2 * LEAF + 1)

        leaf_peers(lambda to, where: remote(g_out.at[to], g_got.at[leaf], g_sem.at[0], g_sem.at[1], where).start())
        mine = pltpu.make_async_copy(g_out.at[leaf], g_got.at[leaf], g_sem.at[1])
        mine.start()
        i = iota((64, 1), 0)
        owner, rank = owner_and_rank(anc_ref[pl.ds(leaf, 1), :], i % 32)
        want = owner * 4.0 + rank * 2.0 + (i // 32).astype(F32)
        take = jnp.where(want == iota((64, 128), 1).astype(F32), 1.0, 0.0).astype(BF16)
        want = (i // 32).astype(F32) * 64.0 + owner * 2.0 + rank
        spread = jnp.where(want == iota((64, 128), 1).astype(F32), 1.0, 0.0).astype(BF16)
        i = iota((128, 1), 0)
        block = listed_block(anc_ref[...], leaf, (i // 2) % 32, i % 2)
        collect_ref[...] = jnp.where(block - 1.0 == iota((128, 128), 1).astype(F32), 1.0, 0.0)
        own = own_ref[...]
        blank = jnp.zeros((192, 64), BF16)
        keys[0, 0:192, :] = jnp.concatenate([own, blank], axis=1)
        keys[1, 0:192, :] = pltpu.roll(jnp.concatenate([own, blank], axis=1).astype(F32), 64, 1).astype(BF16)
        causal = jnp.where(iota((192, 192), 0) <= iota((192, 192), 1), 0.0, -1e30)
        for c in range(4):
            own_scores(c, causal)
        others = pl.ds(0, LEAF - 1)
        remote(g_out.at[others], g_got, g_sem.at[0], g_sem.at[1], right).wait_send()
        remote(g_out, g_got, g_sem.at[0], g_sem.at[1], right).wait_recv()
        for b in range(LEAF):
            g_tall[4 * b:4 * b + 4, :] = g_got[b].astype(F32)
        slabs[y] = dot(take, g_tall[...].astype(BF16), 1, 0).astype(BF16)

        def hop(k, slab, half, where):
            part = slabs.at[slab, pl.ds(32 * half, 32)]
            return remote(part, part, ring_send.at[k], ring_recv.at[k], where)

        up, down, far = lax.rem(y + 3, 4), lax.rem(y + 1, 4), lax.rem(y + 2, 4)
        ring = [hop(0, y, 0, right), hop(1, y, 1, left), hop(2, y, 1, right), hop(3, y, 0, left)]
        for copy in ring:
            copy.start()
        hop(0, up, 0, right).wait_recv()
        ring.append(hop(4, up, 0, right))
        ring[4].start()
        hop(1, down, 1, left).wait_recv()
        ring.append(hop(5, down, 1, left))
        ring[5].start()
        hop(2, up, 1, right).wait_recv()
        hop(3, down, 0, left).wait_recv()
        for n, k in enumerate((0, 1, 3)):
            keys[0, 192 + 64 * n:256 + 64 * n, :] = slabs[lax.rem(y + k, 4)]
        shifted(192, 384)
        for c in range(4):
            near_scores(c)
        hop(4, far, 0, right).wait_recv()
        hop(5, far, 1, left).wait_recv()
        keys[0, 384:448, :] = slabs[far]
    else:
        own = own_ref[...]
        blank = jnp.zeros((192, 64), BF16)
        keys[0, 0:192, :] = jnp.concatenate([own, blank], axis=1)
        keys[1, 0:192, :] = pltpu.roll(jnp.concatenate([own, blank], axis=1).astype(F32), 64, 1).astype(BF16)
        causal = jnp.where(iota((192, 192), 0) <= iota((192, 192), 1), 0.0, -1e30)
        for c in range(4):
            own_scores(c, causal)
        keys[0, 192:320, :] = trunk_ref[0:128, :]
        keys[0, 320:384, :] = trunk_ref[192:256, :]
        shifted(192, 384)
        for c in range(4):
            near_scores(c)
        keys[0, 384:448, :] = trunk_ref[128:192, :]
    shifted(384, 448)

    def last_scores(c):
        u, par = chunks[c]
        return (dot(keys[par, 384:448, :], q_of(u, par), 1, 1) + live(64),
                dot(keys[0, 384:448, 0:512], do_of(u, par), 1, 1))

    ahead = last_scores(0)
    for c in range(4):
        u, par = chunks[c]
        sl, dpl = ahead
        if c < 3:
            ahead = last_scores(c + 1)
        tops = [stats[c, 3 * part:3 * part + 1, :] for part in range(2)]
        m = jnp.maximum(jnp.maximum(tops[0], tops[1]), jnp.max(sl, axis=0, keepdims=True))
        el = jnp.exp2((sl - m) * (SCALE * LOG2E))
        total, delta = jnp.sum(el, axis=0, keepdims=True), jnp.sum(el * dpl, axis=0, keepdims=True)
        factor = [jnp.exp2((top - m) * (SCALE * LOG2E)) for top in tops]
        for part in range(2):
            total = total + factor[part] * stats[c, 3 * part + 1:3 * part + 2, :]
            delta = delta + factor[part] * stats[c, 3 * part + 2:3 * part + 3, :]
        inv = 1.0 / total
        delta = delta * inv
        stats[c, 6:7, :] = factor[0] * inv
        stats[c, 7:8, :] = delta
        pb = eown[c, 192:384, :] * (factor[1] * inv)
        prob[c, 192:384, :] = pb.astype(BF16)
        ds[c, 192:384, :] = (pb * (dpown[c, 192:384, :] - delta)).astype(BF16)
        pb = el * inv
        prob[c, 384:448, :] = pb.astype(BF16)
        ds[c, 384:448, :] = (pb * (dpl - delta)).astype(BF16)
        dk = dot(ds[c, 192:448, :], q_of(u, par), 1, 0)
        dv = dot(prob[c, 192:448, :], do_of(u, par), 1, 0)
        if u == 0:
            acc_k[par, 192:448, :] = dk
        else:
            acc_k[par, 192:448, :] += dk
        if c == 0:
            acc_v[192:448, :] = dv
        else:
            acc_v[192:448, :] += dv

    def merged(lo, n):
        dk = (acc_k[0, lo:lo + n, :] + pltpu.roll(acc_k[1, lo:lo + n, :], 576, 1)) * SCALE
        return jnp.concatenate([dk[:, 0:512] + acc_v[lo:lo + n, :], dk[:, 512:WIDE]], axis=1)

    for at, k in enumerate((0, 1, 3, 2)):
        for half in range(2):
            x_far[k, half] = merged(192 + 64 * at + 32 * half, 32).astype(BF16)

    def ring_start(x, mid, send_sem, recv_sem):
        copies = [
            remote(x(2, 0), mid.at[0], send_sem.at[0], recv_sem.at[0], right),
            remote(x(2, 1), mid.at[1], send_sem.at[1], recv_sem.at[1], left),
            remote(x(1, 1), mid.at[2], send_sem.at[2], recv_sem.at[2], right),
            remote(x(3, 0), mid.at[3], send_sem.at[3], recv_sem.at[3], left),
        ]
        for copy in copies:
            copy.start()
        return copies

    def ring_pass(copies, value, mid, through, send_sem, recv_sem):
        for side, k in ((0, 1), (1, 3)):
            copies[side].wait_recv()
            through[side] = (value(k, side) + mid[side].astype(F32)).astype(BF16)
            copy = remote(through.at[side], mid.at[4 + side], send_sem.at[4 + side], recv_sem.at[4 + side],
                          (right, left)[side])
            copy.start()
            copies.append(copy)

    def ring_sum(copies, value, mid):
        for k in range(2, 6):
            copies[k].wait_recv()
        return [value(0, half) + mid[4 + half].astype(F32) + mid[3 - half].astype(F32) for half in range(2)]

    if comm:
        far_copies = ring_start(lambda k, half: x_far.at[k, half], r_far, far_send, far_recv)

    def own_keys(c):
        u, par = chunks[c]
        pb = eown[c, 0:192, :] * stats[c, 6:7, :]
        score = (pb * (dpown[c, 0:192, :] - stats[c, 7:8, :])).astype(BF16)
        ds[c, 0:192, :] = score
        dk = dot(score, q_of(u, par), 1, 0)
        dv = dot(pb.astype(BF16), do_of(u, par), 1, 0)
        if u == 0:
            acc_k[par, 0:192, :] = dk
        else:
            acc_k[par, 0:192, :] += dk
        if c == 0:
            acc_v[0:192, :] = dv
        else:
            acc_v[0:192, :] += dv

    def own_done():
        for h in range(8):
            x_own[h] = merged(24 * h, 24).astype(BF16)

    def far_value(k, half):
        return x_far[k, half].astype(F32)

    def own_at(k, half):
        return half * 4 + lax.rem(y + k, 4)

    def own_value(k, half):
        return x_own[own_at(k, half)].astype(F32)

    def d_query(u):
        even = dot(ds[2 * u], keys[0], 0, 0) * SCALE
        odd = dot(ds[2 * u + 1], keys[1], 0, 0) * SCALE
        for n in range(4):
            r = slice(192 * n, 192 * n + 192)
            at = 1152 * n
            dq_out[u, :, at:at + 512] = even[r, 0:512].astype(BF16)
            dq_out[u, :, at + 512:at + 640] = (even[r, 512:640] + odd[r, 0:128]).astype(BF16)
            dq_out[u, :, at + 640:at + 1152] = odd[r, 128:640].astype(BF16)
        copy = pltpu.make_async_copy(dq_out.at[u], dq_ref.at[:, pl.ds(4608 * u, 4608)], store_sem.at[u])
        copy.start()
        return copy

    for c in range(4):
        own_keys(c)
    own_done()
    if comm:
        own_copies = ring_start(lambda k, half: x_own.at[own_at(k, half)], r_own, own_send, own_recv)
        ring_pass(far_copies, far_value, r_far, m_far, far_send, far_recv)
        stores = [d_query(0)]
        ring_pass(own_copies, own_value, r_own, m_own, own_send, own_recv)
        sums = ring_sum(far_copies, far_value, r_far)
        rows = dot(spread, jnp.concatenate(sums, axis=0).astype(BF16), 0, 0)
        for d in range(2 * LEAF):
            t_out[d] = rows[2 * d:2 * d + 2].astype(BF16)

        plane_peers(lambda to, where: remote(t_out.at[to], t_got.at[me], t_sem.at[0], t_sem.at[1], where).start())
        mine = pltpu.make_async_copy(t_out.at[me], t_got.at[me], t_sem.at[1])
        mine.start()
        sums = ring_sum(own_copies, own_value, r_own)
        for half in range(2):
            pair[half] = sums[half].astype(BF16)
        pair_out = remote(pair.at[1 - deep], pair_in, pair_sem.at[0], pair_sem.at[1], across)
        pair_out.start()
        stores.append(d_query(1))
        others = pl.ds(0, 2 * LEAF - 1)
        remote(t_out.at[others], t_got, t_sem.at[0], t_sem.at[1], right).wait_send()
        remote(t_out, t_got, t_sem.at[0], t_sem.at[1], right).wait_recv()
        for d in range(2 * LEAF):
            spare_ref[2 * d:2 * d + 2, :] = t_got[d].astype(F32)
        for copy in ring + far_copies + own_copies:
            copy.wait_send()
        for copy in stores:
            copy.wait()
        pair_out.wait()
        kept = jnp.where(deep == 0, sums[0], sums[1])
        branch_ref[...] = kept + pair_in[...].astype(F32)
    else:
        stores = [d_query(0), d_query(1)]
        spare_ref[...] = x_far[...]
        branch_ref[...] = x_own[...]
        for copy in stores:
            copy.wait()


def fused_call(comm, ancestors, count, own, trunk, q, do):
    if comm:
        small = (pltpu.VMEM((24, WIDE), F32), pltpu.VMEM((128, WIDE), F32))
    else:
        small = (pltpu.VMEM((8, 24, WIDE), BF16), pltpu.VMEM((4, 2, 32, WIDE), BF16))
    vmem, hbm = pl.BlockSpec(memory_space=pltpu.VMEM), pl.BlockSpec(memory_space=pltpu.HBM)
    dma = pltpu.SemaphoreType.DMA
    return pl.pallas_call(
        functools.partial(fused, comm),
        out_shape=(pltpu.VMEM((192, 9216), BF16),) + small + (pltpu.VMEM((128, 128), F32),),
        in_specs=[hbm] * 6,
        out_specs=(pl.BlockSpec(memory_space=pl.ANY),) + (vmem,) * 3,
        scratch_shapes=[
            pltpu.VMEM((LEAF, LEAF), jnp.int32),
            pltpu.SMEM(count.shape, jnp.int32),
            pltpu.VMEM(own.shape, BF16),
            pltpu.VMEM(trunk.shape, BF16),
            dma((4,)),
            pltpu.VMEM((2, 1536, WIDE), BF16),
            pltpu.VMEM((2, 1536, 512), BF16),
            pltpu.VMEM((2, 448, WIDE), BF16),
            pltpu.VMEM((4, 384, 768), F32),
            pltpu.VMEM((4, 384, 768), F32),
            pltpu.VMEM((4, 8, 768), F32),
            pltpu.VMEM((4, 448, 768), BF16),
            pltpu.VMEM((4, 448, 768), BF16),
            pltpu.VMEM((2, 448, WIDE), F32),
            pltpu.VMEM((448, 512), F32),
            pltpu.VMEM((2, 192, 4608), BF16),
            pltpu.VMEM((LEAF, 4, WIDE), BF16),
            pltpu.VMEM((LEAF, 4, WIDE), BF16),
            pltpu.VMEM((128, WIDE), F32),
            pltpu.VMEM((4, 64, WIDE), BF16),
            pltpu.VMEM((4, 2, 32, WIDE), BF16),
            pltpu.VMEM((8, 24, WIDE), BF16),
            pltpu.VMEM((6, 32, WIDE), BF16),
            pltpu.VMEM((6, 24, WIDE), BF16),
            pltpu.VMEM((2, 32, WIDE), BF16),
            pltpu.VMEM((2, 24, WIDE), BF16),
            pltpu.VMEM((2, 24, WIDE), BF16),
            pltpu.VMEM((24, WIDE), BF16),
            pltpu.VMEM((2 * LEAF, 2, WIDE), BF16),
            pltpu.VMEM((2 * LEAF, 2, WIDE), BF16),
            dma((8,)), dma((2,)), dma((2,)), dma((6,)), dma((6,)), dma((6,)), dma((6,)), dma((6,)), dma((6,)),
            dma((2,)), dma((2,)),
        ],
        compiler_params=pltpu.CompilerParams(
            collective_id=0, has_side_effects=True, vmem_limit_bytes=VMEM_LIMIT
        ) if comm else pltpu.CompilerParams(vmem_limit_bytes=VMEM_LIMIT),
        name="backward",
    )(ancestors, count, own, trunk, q, do)


def finish(grad_ref, rows_ref, sum_ref, collect_ref, dq_hbm, branch_hbm, trunk_hbm, branch, trunk, sem):
    copies = [
        pltpu.make_async_copy(grad_ref, dq_hbm, sem.at[0]),
        pltpu.make_async_copy(branch, branch_hbm, sem.at[1]),
        pltpu.make_async_copy(trunk, trunk_hbm, sem.at[2]),
    ]
    copies[0].start()
    branch[...] = sum_ref[:, 0:576]
    copies[1].start()
    total = dot(collect_ref[...].astype(BF16), rows_ref[...].astype(BF16), 0, 0)
    for b in range(16):
        trunk[b] = total[b:b + 1, 0:576]
    copies[2].start()
    for copy in copies:
        copy.wait()


def finish_call(grad, rows, total, collect):
    return pl.pallas_call(
        finish,
        out_shape=(
            jax.ShapeDtypeStruct((192, 9216), BF16),
            jax.ShapeDtypeStruct((24, 576), F32),
            jax.ShapeDtypeStruct((16, 1, 576), F32),
        ),
        in_specs=[pl.BlockSpec(memory_space=pltpu.VMEM)] * 4,
        out_specs=(pl.BlockSpec(memory_space=pltpu.HBM),) * 3,
        scratch_shapes=[
            pltpu.VMEM((24, 576), F32),
            pltpu.VMEM((16, 1, 576), F32),
            pltpu.SemaphoreType.DMA((3,)),
        ],
        compiler_params=pltpu.CompilerParams(vmem_limit_bytes=16 * 2**20),
        name="finish",
    )(grad, rows, total, collect)


def local(queries, d_out, branch_latent, trunk_latent, ancestors, anc_count):
    ancestors, anc_count = (pltpu.with_memory_space_constraint(a, pltpu.HBM) for a in (ancestors, anc_count))
    grad, total, rows, collect = fused_call(True, ancestors, anc_count, branch_latent, trunk_latent, queries, d_out)
    return finish_call(grad, rows, total, collect)


def solution(mesh):
    return jax.shard_map(
        local,
        mesh=mesh,
        in_specs=(P("leaf", "head"), P("leaf", "head"), P("leaf", None), P("leaf", None, None), P(), P()),
        out_specs=(P("leaf", "head"), P(("leaf", "head"), None), P("leaf", "head", None)),
        check_vma=False,
    )
```
